32 devices in a mesh: seq: 8 (over z, core), chan: 4 (over y, x).
Axes of the slice: x: 2, y: 2, z: 4, core: 2. Of those that a mesh axis runs over, the one named last changes fastest.
Arguments:
- gate_raw: bfloat16 [8, 2048, 2048], P('seq', None, 'chan'), may hold values from -50 to 50
- value_raw: bfloat16 [8, 2048, 2048], P('seq', None, 'chan'), may hold values from -50 to 50
- filter_gate: float32 [7, 2048], P(None, 'chan'), may hold values from -3 to 3
- filter_value: float32 [7, 2048], P(None, 'chan'), may hold values from -3 to 3
- teacher: float32 [8, 2048, 2048], P('seq', 'chan'), may hold values from -0.25 to 1, as said below
Outputs:
- grad_gate_raw: bfloat16 [8, 2048, 2048], P('seq', None, 'chan')
- grad_value_raw: bfloat16 [8, 2048, 2048], P('seq', None, 'chan')
- grad_filter_gate: float32 [7, 2048], P(None, 'chan')
- grad_filter_value: float32 [7, 2048], P(None, 'chan')
The draws below stay inside these ranges and needn't reach their ends.
Inputs may be any that keep to these rules, and one draw needn't show every extreme that they name: teacher[s] is symmetric for each of the 8 sequences, with ones on its diagonal.
All inputs are finite; a program needn't handle non-finite values.
Results may differ from the reference program's by a relative error of at most 0.0059.
Values may be sent and summed in bfloat16 or wider, within the bound.
A program may use at most 128 MiB of HBM per device.

```python
import math
import jax
import jax.numpy as jnp
from jax import lax

D = 2048
TAPS = 7
LEN = 2048
SEQS = 8


def scaled_field(key):
    key_base, key_rows, key_chan = jax.random.split(key, 3)
    extent = (SEQS, LEN, D)
    values = jnp.clip(jax.random.normal(key_base, extent, jnp.float32), -4.0, 4.0)
    ramp_span = 0.25 * math.log(3.0)
    half_decade = 0.5 * math.log(10.0)
    row_scale = jnp.exp(jax.random.uniform(key_rows, (SEQS, LEN, 1), jnp.float32, 0.0, half_decade))
    channel_ramp = jnp.arange(D, dtype=jnp.float32) * (ramp_span / D)
    chan_scale = jnp.exp(channel_ramp + jax.random.uniform(key_chan, (D,), jnp.float32, -0.22, 0.22))
    return (values * row_scale * chan_scale).astype(jnp.bfloat16)


def draw_gate_raw(key, part):
    return scaled_field(jax.random.fold_in(key, 17))


def draw_value_raw(key, part):
    return scaled_field(jax.random.fold_in(key, 23))


def draw_teacher(key, part):
    extent = (SEQS, LEN, LEN)
    noise_key = jax.random.fold_in(key, 41)
    raw_values = jnp.clip(jax.random.normal(noise_key, extent, jnp.float32), -4.0, 4.0) * 0.05
    symmetric = 0.5 * (raw_values + jnp.swapaxes(raw_values, 1, 2))
    position = jnp.arange(LEN)
    diagonal = position[:, None] == position[None, :]
    return jnp.where(diagonal, 1.0, symmetric).astype(jnp.float32)


def block_levels(own_key, dims, cuts, smallest, largest):
    level, own = 1.0, jax.random.fold_in(own_key, 6)
    for axis_at, parts in cuts:
        draws = jnp.exp(jax.random.uniform(jax.random.fold_in(own, axis_at), (parts,), jnp.float32, smallest / len(cuts), largest / len(cuts)))
        level = level * jnp.repeat(draws, dims[axis_at] // parts).reshape([-1 if axis == axis_at else 1 for axis in range(len(dims))])
    return level


def gaussian(own_key, shape, width, most, pieces=(), kind=jnp.bfloat16):
    drawn = width * jax.random.normal(own_key, shape, jnp.float32)
    if pieces:
        drawn = drawn * block_levels(own_key, shape, pieces, -0.22, 0.18)
    return jnp.clip(drawn, -most, most).astype(kind)


def setup_inputs(seed: int = 0) -> dict:
    key_list = jax.random.split(jax.random.key(seed), 6)
    return {
        "gate_raw": draw_gate_raw(jax.random.fold_in(key_list[5], 71), 0),
        "value_raw": draw_value_raw(jax.random.fold_in(key_list[5], 71), 0),
        "filter_gate": gaussian(key_list[2], (TAPS, D), 0.5, 3.0, ((1, 4),), jnp.float32),
        "filter_value": gaussian(key_list[3], (TAPS, D), 0.5, 3.0, ((1, 4),), jnp.float32),
        "teacher": draw_teacher(jax.random.fold_in(key_list[5], 71), 0),
    }


epsilon = 1e-06

def causal_conv(signal, weights):
    length = signal.shape[0]
    padded = jnp.pad(signal.astype(jnp.float32), ((TAPS - 1, 0), (0, 0)))
    summed = jnp.zeros(signal.shape, jnp.float32)
    for tap_index in range(TAPS):
        summed = summed + weights[tap_index] * padded[TAPS - 1 - tap_index:TAPS - 1 - tap_index + length]
    return summed

def adjoint_conv(upstream, weights):
    length = upstream.shape[0]
    padded = jnp.pad(upstream, ((0, TAPS - 1), (0, 0)))
    summed = jnp.zeros(upstream.shape, jnp.float32)
    for tap_index in range(TAPS):
        summed = summed + weights[tap_index] * padded[tap_index:tap_index + length]
    return summed

def tap_sums(upstream, signal):
    length = signal.shape[0]
    padded = jnp.pad(signal.astype(jnp.float32), ((TAPS - 1, 0), (0, 0)))
    return jnp.stack([lax.optimization_barrier(jnp.sum(upstream * padded[TAPS - 1 - tap_index:TAPS - 1 - tap_index + length], axis=0)) for tap_index in range(TAPS)])

def reference(gate_raw, value_raw, filter_gate, filter_value, teacher):
    factor = 16.0 / math.sqrt(LEN)

    def one_sequence(inputs):
        gate_seq, value_seq, teacher_seq = inputs
        gate_conv = causal_conv(gate_seq, filter_gate)
        value_conv = causal_conv(value_seq, filter_value)
        hidden = (gate_conv * value_conv).astype(jnp.bfloat16)
        hidden_f = hidden.astype(jnp.float32)
        inv_rms = lax.rsqrt(lax.optimization_barrier(jnp.sum(hidden_f * hidden_f, axis=1, keepdims=True)) / D + epsilon)
        normed_f = hidden_f * inv_rms
        normed = normed_f.astype(jnp.bfloat16)
        similarity = jnp.dot(normed, normed.T, preferred_element_type=jnp.float32) / D
        residue = (factor * (similarity - teacher_seq)).astype(jnp.bfloat16)
        normed_grad = jnp.dot(residue, normed, preferred_element_type=jnp.float32)
        projection = lax.optimization_barrier(jnp.sum(normed_f * normed_grad, axis=1, keepdims=True)) / D
        hidden_grad = inv_rms * (normed_grad - normed_f * projection)
        gate_conv_grad = hidden_grad * value_conv
        value_conv_grad = hidden_grad * gate_conv
        grad_gate = adjoint_conv(gate_conv_grad, filter_gate).astype(jnp.bfloat16)
        grad_value = adjoint_conv(value_conv_grad, filter_value).astype(jnp.bfloat16)
        return (grad_gate, grad_value, tap_sums(gate_conv_grad, gate_seq), tap_sums(value_conv_grad, value_seq))
    grad_gate, grad_value, gate_taps, value_taps = lax.map(one_sequence, (gate_raw, value_raw, teacher))
    norm_factor = 1.0 / math.sqrt(SEQS * LEN)
    return (grad_gate, grad_value, lax.optimization_barrier(jnp.sum(gate_taps, axis=0)) * norm_factor, lax.optimization_barrier(jnp.sum(value_taps, axis=0)) * norm_factor)
```

```python
import functools
import math

import jax
import jax.numpy as jnp
from jax import lax
from jax.experimental import pallas as pl
from jax.experimental.pallas import tpu as pltpu
from jax.sharding import PartitionSpec as P

epsilon = 1e-06
PAD = 16
TILE = 64
BLK = 256
MESH = pl.DeviceIdType.MESH


def stripe_kernel(
    groups, rings, taps, norm_factor,
    gate_in, value_in, filter_gate, filter_value, teacher_in,
    gate_out, value_out, gate_taps, value_taps,
    raw_g, raw_v, conv_g, conv_v, held, teach, own_n, block_n, total, outgoing, hgrad,
    sums, mine, others,
    in_sem, send_sem, recv_sem, a2a_send, a2a_recv, tap_send, tap_recv,
):
    length, width = gate_in.shape[1:]
    stripe = length // groups
    full = width * groups
    factor = 16.0 / math.sqrt(length)
    tile = min(TILE, stripe)
    lanes = [slice(k, min(k + 128, width)) for k in range(0, width, 128)]
    f32, bf16 = jnp.float32, jnp.bfloat16
    me, ring = lax.axis_index("chan"), lax.axis_index("seq")
    base_at, slot, proc = me, me, ring

    def rows_of(chunk, size=stripe, start=0):
        return pl.ds(pl.multiple_of(chunk * stripe + start, math.gcd(stripe, start) if start else stripe), size)

    in_copies = []
    for c in range(groups):
        span = pl.ds(c * stripe, stripe)
        dest = pl.ds(PAD + c * stripe, stripe)
        for k, (src, dst) in enumerate(((gate_in, raw_g), (value_in, raw_v))):
            in_copies.append(pltpu.make_async_copy(src.at[0, span], dst.at[dest], in_sem.at[k, c]))
    for copy in in_copies:
        copy.start()
    teach_copy = pltpu.make_async_copy(teacher_in.at[0], teach, in_sem.at[2, 0])
    teach_copy.start()

    barrier = pltpu.get_barrier_semaphore()
    for step in range(1, groups):
        pl.semaphore_signal(barrier, inc=1, device_id=(ring, lax.rem(me + step, groups)), device_id_type=MESH)
    greeted = groups + rings - 2
    for step in range(1, rings):
        pl.semaphore_signal(barrier, inc=1, device_id=(lax.rem(ring + step, rings), me), device_id_type=MESH)

    raw_g[0:PAD] = jnp.zeros((PAD, width), bf16)
    raw_v[0:PAD] = jnp.zeros((PAD, width), bf16)
    conv_g[length:] = jnp.zeros((PAD, width), f32)
    conv_v[length:] = jnp.zeros((PAD, width), f32)
    hgrad[length:] = jnp.zeros((PAD, width), bf16)
    sums[...] = jnp.zeros(sums.shape, f32)
    total[...] = jnp.zeros(total.shape, f32)
    for copy in in_copies:
        copy.wait()

    def conv_chunk(chunk):
        def body(i, _):
            base = pl.multiple_of(chunk * stripe + i * tile, tile)
            for lane in lanes:
                made = []
                for raw, weights, store in ((raw_g, filter_gate, conv_g), (raw_v, filter_value, conv_v)):
                    window = raw[pl.ds(base, tile + PAD), lane].astype(f32)
                    out = weights[0:1, lane] * window[PAD:]
                    for j in range(1, taps):
                        out = out + weights[j : j + 1, lane] * pltpu.roll(window, j, 0)[PAD:]
                    store[pl.ds(base, tile), lane] = out
                    made.append(out)
                held[slot, pl.ds(base, tile), lane] = (made[0] * made[1]).astype(bf16)
            return 0

        lax.fori_loop(0, stripe // tile, body, 0)

    def gather_copy(source, target, chunk, to, send):
        rows = rows_of(chunk)
        return pltpu.make_async_remote_copy(
            src_ref=held.at[source, rows], dst_ref=held.at[target, rows],
            send_sem=send, recv_sem=recv_sem.at[target, chunk],
            device_id=to, device_id_type=MESH,
        )

    def arrived(source, chunk):
        gather_copy(source, source, chunk, (ring, me), send_sem.at[0, 0]).wait_recv()

    for c in range(groups):
        conv_chunk(c)
    pl.semaphore_wait(barrier, greeted)

    def send_all(copy_do):
        def body(i, _):
            chunk, step = i // (groups - 1), 1 + lax.rem(i, groups - 1)
            copy_do(gather_copy(me, me, chunk, (ring, lax.rem(me + step, groups)), send_sem.at[step, chunk]))
            return 0

        lax.fori_loop(0, groups * (groups - 1), body, 0)

    send_all(lambda copy: copy.start())

    def wait_chunk(chunk):
        def body(step, _):
            arrived(lax.rem(me + step, groups), chunk)
            return 0

        lax.fori_loop(1, groups, body, 0)

    norm_tile = min(32, stripe)

    def scale_of(base):
        squares = jnp.zeros((norm_tile, width), f32)
        for g in range(groups):
            block = held[g, pl.ds(base, norm_tile)].astype(f32)
            squares = squares + block * block
        return lax.rsqrt(jnp.sum(squares, axis=1, keepdims=True) / full + epsilon)

    def normalize(chunk, dest):
        def body(i, _):
            base = pl.multiple_of(chunk * stripe + i * norm_tile, norm_tile)
            inverse = scale_of(base)
            for g in range(groups):
                block = held[g, pl.ds(base, norm_tile)].astype(f32)
                dest[pl.ds(pl.multiple_of(i * norm_tile, norm_tile), norm_tile), g * width : (g + 1) * width] = (
                    block * inverse
                ).astype(bf16)
            return 0

        lax.fori_loop(0, stripe // norm_tile, body, 0)

    teach_copy.wait()
    mat = min(256, stripe)

    def gram_chunk(t, _):
        chunk = lax.rem(me + t, groups)
        wait_chunk(chunk)
        normalize(chunk, block_n)

        @pl.when(t == 0)
        def _():
            own_n[...] = block_n[...]

        def body(m, _):
            rows = pl.ds(pl.multiple_of(m * mat, mat), mat)
            similarity = lax.dot_general(
                own_n[rows], block_n[...], (((1,), (1,)), ((), ())), preferred_element_type=f32
            ) / full
            residue = (factor * (similarity - teach[rows, rows_of(chunk)])).astype(bf16)
            total[rows] += jnp.dot(residue, block_n[...], preferred_element_type=f32)
            return 0

        lax.fori_loop(0, stripe // mat, body, 0)
        return 0

    lax.fori_loop(0, groups, gram_chunk, 0)

    def finish(i, _):
        local = pl.multiple_of(i * norm_tile, norm_tile)
        base = pl.multiple_of(base_at * stripe + i * norm_tile, norm_tile)
        rows = pl.ds(local, norm_tile)
        inverse = scale_of(base)
        inner = jnp.zeros((norm_tile, width), f32)
        for g in range(groups):
            part = slice(g * width, (g + 1) * width)
            inner = inner + held[g, pl.ds(base, norm_tile)].astype(f32) * inverse * total[rows, part]
        projection = jnp.sum(inner, axis=1, keepdims=True) / full
        for g in range(groups):
            part = slice(g * width, (g + 1) * width)
            normed = held[g, pl.ds(base, norm_tile)].astype(f32) * inverse
            outgoing[g, rows] = (inverse * (total[rows, part] - normed * projection)).astype(bf16)
        return 0

    pieces = max(1, min(4, stripe // 128))
    piece = stripe // pieces
    steps = piece // norm_tile

    def exchange(target, p, source_row):
        return pltpu.make_async_remote_copy(
            src_ref=outgoing.at[target, pl.ds(p * piece, piece)],
            dst_ref=hgrad.at[rows_of(source_row, piece, p * piece)],
            send_sem=a2a_send.at[target, p], recv_sem=a2a_recv.at[source_row, p],
            device_id=(proc, target), device_id_type=MESH,
        )

    targets = tuple(lax.rem(me + groups - step, groups) for step in range(1, groups))

    def stay(p):
        hgrad[rows_of(base_at, piece, p * piece)] = outgoing[me, pl.ds(p * piece, piece)]

    for p in reversed(range(pieces)):
        lax.fori_loop(p * steps, (p + 1) * steps, finish, 0)
        for target in targets:
            exchange(target, p, base_at).start()
        stay(p)

    def back_tile(base):
        for k in range(0, width, 128):
            lane = slice(k, min(k + 128, width))
            up = hgrad[pl.ds(base, tile + PAD), lane].astype(f32)
            for b, (conv, raw, weights, store) in enumerate(
                ((conv_v, raw_g, filter_gate, gate_out), (conv_g, raw_v, filter_value, value_out))
            ):
                window = up * conv[pl.ds(base, tile + PAD), lane]
                signal = raw[pl.ds(pl.multiple_of(base + PAD, PAD), tile), lane].astype(f32)
                out = None
                for j in range(taps):
                    shifted = (window if j == 0 else pltpu.roll(window, tile + PAD - j, 0))[:tile]
                    term = weights[j : j + 1, lane] * shifted
                    out = term if out is None else out + term
                    product = shifted * signal
                    folded = product[0:8]
                    for r in range(8, tile, 8):
                        folded = folded + product[r : r + 8]
                    sums[b, j, :, lane] += folded
                store[0, pl.ds(base, tile), lane] = out.astype(bf16)

    tiles = stripe // tile
    per = tiles // pieces
    sources = tuple(lax.rem(me + step, groups) for step in range(groups))
    for p in reversed(range(pieces)):
        for step, source in enumerate(sources):
            def landed(p=p, source=source):
                exchange(source, p, source).wait_recv()

            if step:
                landed()

            def inner_tiles(i, _, source=source):
                back_tile(pl.multiple_of(source * stripe + i * tile, tile))
                return 0

            lax.fori_loop(p * per, (p + 1) * per - (1 if p == pieces - 1 else 0), inner_tiles, 0)

    def last_tiles(c, _):
        back_tile(pl.multiple_of(c * stripe + (tiles - 1) * tile, tile))
        return 0

    lax.fori_loop(0, groups, last_tiles, 0)
    for b in range(2):
        for j in range(taps):
            mine[b, j : j + 1] = jnp.sum(sums[b, j], axis=0, keepdims=True)
        mine[b, taps:] = jnp.zeros((8 - taps, width), f32)

    def tap_copy(to, slot):
        return pltpu.make_async_remote_copy(
            src_ref=mine, dst_ref=others.at[slot], send_sem=tap_send.at[slot], recv_sem=tap_recv.at[slot],
            device_id=(to, me), device_id_type=MESH,
        )

    tap_copies = [tap_copy(lax.rem(ring + step, rings), step) for step in range(1, rings)]
    for copy in tap_copies:
        copy.start()
    summed = [mine[b] for b in range(2)]
    for step, copy in enumerate(tap_copies):
        copy.wait_recv()
        summed = [summed[b] + others[step + 1, b] for b in range(2)]
    gate_taps[...] = summed[0][:taps] * norm_factor
    value_taps[...] = summed[1][:taps] * norm_factor

    for copy in tap_copies:
        copy.wait_send()
    send_all(lambda copy: copy.wait_send())
    for target in targets:
        for p in range(pieces):
            exchange(target, p, base_at).wait_send()


def quad_kernel(
    rings, taps, norm_factor,
    gate_in, value_in, filter_gate, filter_value, teacher_in,
    gate_out, value_out, gate_taps, value_taps,
    raw_g, raw_v, conv_g, conv_v, hid, nrm, teach, perm, keep,
    s1, r1, s2, r2, res, gbuf, hgrad, lane_sums, small, invc,
    sums, mine, others,
    in_sem, s1_send, s1_recv, s2_send, s2_recv, ag_send, ag_recv,
    small_send, small_recv, tap_send, tap_recv,
):
    groups = 4
    length, width = gate_in.shape[1:]
    stripe, full = length // groups, width * groups
    factor = 16.0 / math.sqrt(length)
    blocks = length // BLK
    half, quarter, eighth = BLK // 2, BLK // 4, BLK // 8
    lanes = [slice(k, k + 128) for k in range(0, width, 128)]
    f32, bf16 = jnp.float32, jnp.bfloat16
    me, ring = lax.axis_index("chan"), lax.axis_index("seq")
    x, y = lax.rem(me, 2), me // 2
    across, along, diagonal = me + 1 - 2 * x, lax.rem(me + 2, 4), 3 - me
    offset = [BLK * (l * (l + 1) // 2) for l in range(blocks)]

    def rows(start, size, unit=None):
        return pl.ds(pl.multiple_of(start, unit or size), size)

    def push(src, dst, send, recv, to):
        return pltpu.make_async_remote_copy(
            src_ref=src, dst_ref=dst, send_sem=send, recv_sem=recv,
            device_id=(ring, to), device_id_type=MESH,
        )

    in_copies = []
    for l in range(blocks):
        for k, (src, dst) in enumerate(((gate_in, raw_g), (value_in, raw_v))):
            in_copies.append(pltpu.make_async_copy(
                src.at[0, pl.ds(l * BLK, BLK)], dst.at[pl.ds(PAD + l * BLK, BLK)], in_sem.at[k, l]
            ))
    for copy in in_copies:
        copy.start()
    teach_copy = pltpu.make_async_copy(teacher_in.at[0], teach, in_sem.at[2, 0])
    teach_copy.start()

    barrier = pltpu.get_barrier_semaphore()
    for to in (across, along, diagonal):
        pl.semaphore_signal(barrier, inc=1, device_id=(ring, to), device_id_type=MESH)
    for step in range(1, rings):
        pl.semaphore_signal(barrier, inc=1, device_id=(lax.rem(ring + step, rings), me), device_id_type=MESH)

    raw_g[0:PAD] = jnp.zeros((PAD, width), bf16)
    raw_v[0:PAD] = jnp.zeros((PAD, width), bf16)
    conv_g[length:] = jnp.zeros((PAD, width), f32)
    conv_v[length:] = jnp.zeros((PAD, width), f32)
    hgrad[length:] = jnp.zeros((PAD, width), f32)
    sums[...] = jnp.zeros(sums.shape, f32)

    def share(kind, l):
        small[kind, me, l] = jnp.broadcast_to(jnp.sum(lane_sums[...].T, axis=0, keepdims=True), (8, BLK))
        for k, to in enumerate((across, along, diagonal)):
            here = small.at[kind, me, l]
            push(here, here, small_send.at[kind, k, l], small_recv.at[kind, me, l], to).start()

    def total(kind, l):
        for o in (across, along, diagonal):
            there = small.at[kind, o, l]
            push(there, there, small_send.at[kind, 0, l], small_recv.at[kind, o, l], o).wait_recv()
        return small[kind, 0, l, 0:1] + small[kind, 1, l, 0:1] + small[kind, 2, l, 0:1] + small[kind, 3, l, 0:1]

    def column(row):
        return jnp.broadcast_to(row, (128, BLK)).T

    def conv(l):
        in_copies[2 * l].wait()
        in_copies[2 * l + 1].wait()

        def body(i, _):
            base = pl.multiple_of(l * BLK + i * TILE, TILE)
            squares = jnp.zeros((TILE, 128), f32)
            for lane in lanes:
                made = []
                for raw, weights, store in ((raw_g, filter_gate, conv_g), (raw_v, filter_value, conv_v)):
                    window = raw[pl.ds(base, TILE + PAD), lane].astype(f32)
                    out = weights[0:1, lane] * window[PAD:]
                    for j in range(1, taps):
                        out = out + weights[j : j + 1, lane] * pltpu.roll(window, j, 0)[PAD:]
                    store[pl.ds(base, TILE), lane] = out
                    made.append(out)
                hidden = (made[0] * made[1]).astype(bf16)
                hid[pl.ds(base, TILE), lane] = hidden
                hidden = hidden.astype(f32)
                squares = squares + hidden * hidden
            lane_sums[pl.ds(pl.multiple_of(i * TILE, TILE), TILE)] = squares
            return 0

        lax.fori_loop(0, BLK // TILE, body, 0)

    def normalize(l):
        invc[pl.ds(l * BLK, BLK)] = column(lax.rsqrt(total(0, l) / full + epsilon))

        def body(i, _):
            base = pl.multiple_of(l * BLK + i * TILE, TILE)
            inverse = invc[pl.ds(base, TILE)]
            for lane in lanes:
                nrm[pl.ds(base, TILE), lane] = (hid[pl.ds(base, TILE), lane].astype(f32) * inverse).astype(bf16)
            return 0

        lax.fori_loop(0, BLK // TILE, body, 0)

    pieces = (quarter * (1 - x), half + quarter * (1 - y), quarter * x, half + quarter * y)

    def stage_one(l):
        span = pl.ds(offset[l], (l + 1) * BLK)
        for k, to in enumerate((across, along)):
            yield push(s1.at[k, :, span], r1.at[k, :, span], s1_send.at[k, l], s1_recv.at[k, l], to)

    def stage_two(l):
        span = pl.ds(offset[l], (l + 1) * BLK)
        for k, to in enumerate((across, along)):
            yield push(s2.at[k, :, span], r2.at[k, :, span], s2_send.at[k, l], s2_recv.at[k, l], to)

    def gram(l):
        for k, piece in enumerate(pieces):
            perm[k * quarter : (k + 1) * quarter] = nrm[rows(l * BLK + piece, quarter)]
        top = (l * BLK) % stripe
        held = jnp.where(me == (l * BLK) // stripe, 1.0, 0.0)

        def body(j, _):
            part = lax.dot_general(
                perm[...], nrm[rows(j * BLK, BLK)], (((1,), (1,)), ((), ())), preferred_element_type=f32
            ) / full
            cols = rows(offset[l] + j * BLK, BLK)
            for k, piece in enumerate(pieces):
                target = teach[rows(top + piece, quarter), rows(j * BLK, BLK)]
                apart = part[k * quarter : (k + 1) * quarter] - held * target
                if k < 2:
                    s1[k, :, cols] = apart.astype(bf16)
                else:
                    keep[k - 2, :, cols] = apart
            return 0

        lax.fori_loop(0, l + 1, body, 0)
        for copy in stage_one(l):
            copy.start()

    turns = ((0, y), (1, x))

    def combine(l):
        for copy in stage_one(l):
            copy.wait_recv()

        def body(j, _):
            cols = rows(offset[l] + j * BLK, BLK)
            for k, own in turns:
                away = rows(eighth * (1 - own), eighth)
                s2[1 - k, :, cols] = (keep[k, away, cols] + r1[k, away, cols].astype(f32)).astype(bf16)
            return 0

        lax.fori_loop(0, l + 1, body, 0)
        for copy in stage_two(l):
            copy.start()

    def place(l, k, px, py):
        return l * BLK + (quarter * px + eighth * py if k == 0 else half + quarter * py + eighth * px)

    def residue(l):
        for copy in stage_two(l):
            copy.wait_recv()

        def body(j, _):
            cols = rows(offset[l] + j * BLK, BLK)
            for k, own in turns:
                here = rows(eighth * own, eighth)
                apart = keep[k, here, cols] + r1[k, here, cols].astype(f32) + r2[1 - k, :, cols].astype(f32)
                res[rows(place(l, k, x, y), eighth), rows(j * BLK, BLK)] = (factor * apart).astype(bf16)
            return 0

        lax.fori_loop(0, l + 1, body, 0)

    def gather(l, slot, k, px, py, to):
        area = res.at[rows(place(l, k, px, py), eighth), pl.ds(0, (l + 1) * BLK)]
        return push(area, area, ag_send.at[slot, l], ag_recv.at[slot, l], to)

    def own_rows(l):
        return (
            gather(l, 0, 0, x, y, across), gather(l, 3, 1, x, y, along),
            gather(l, 1, 1, x, y, across), gather(l, 2, 0, x, y, along),
        )

    def relays(l):
        return gather(l, 4, 0, 1 - x, y, along), gather(l, 5, 1, x, 1 - y, across)

    def relay(l):
        first, second = relays(l)
        gather(l, 0, 0, 1 - x, y, across).wait_recv()
        first.start()
        gather(l, 3, 1, x, 1 - y, along).wait_recv()
        second.start()

    def landed(l):
        gather(l, 1, 1, 1 - x, y, across).wait_recv()
        gather(l, 2, 0, x, 1 - y, along).wait_recv()
        gather(l, 4, 0, 1 - x, 1 - y, along).wait_recv()
        gather(l, 5, 1, 1 - x, 1 - y, across).wait_recv()

    def multiply(l):
        start, stop = l * BLK, (l + 1) * BLK
        out = jnp.dot(res[start:stop, 0:stop], nrm[0:stop], preferred_element_type=f32)
        if stop < length:
            out = out + lax.dot_general(
                res[stop:length, start:stop], nrm[stop:length], (((0,), (0,)), ((), ())), preferred_element_type=f32
            )
        gbuf[l % 2] = out

        def body(i, _):
            local = rows(i * TILE, TILE)
            at = rows(start + i * TILE, TILE)
            inner = jnp.zeros((TILE, 128), f32)
            for lane in lanes:
                inner = inner + hid[at, lane].astype(f32) * invc[at] * gbuf[l % 2, local, lane]
            lane_sums[local] = inner
            return 0

        lax.fori_loop(0, BLK // TILE, body, 0)
        share(1, l)

    def finish(l):
        lane_sums[...] = column(total(1, l) / full)

        def body(i, _):
            local = rows(i * TILE, TILE)
            at = rows(l * BLK + i * TILE, TILE)
            inverse, projection = invc[at], lane_sums[local]
            for lane in lanes:
                normed = hid[at, lane].astype(f32) * inverse
                hgrad[at, lane] = inverse * (gbuf[l % 2, local, lane] - normed * projection)
            return 0

        lax.fori_loop(0, BLK // TILE, body, 0)

    def back(l):
        def body(i, _):
            base = pl.multiple_of(l * BLK + i * TILE, TILE)
            for lane in lanes:
                up = hgrad[pl.ds(base, TILE + PAD), lane]
                for b, (conv_by, raw, weights, store) in enumerate(
                    ((conv_v, raw_g, filter_gate, gate_out), (conv_g, raw_v, filter_value, value_out))
                ):
                    window = up * conv_by[pl.ds(base, TILE + PAD), lane]
                    signal = raw[pl.ds(pl.multiple_of(base + PAD, PAD), TILE), lane].astype(f32)
                    out = None
                    for j in range(taps):
                        shifted = (window if j == 0 else pltpu.roll(window, TILE + PAD - j, 0))[:TILE]
                        term = weights[j : j + 1, lane] * shifted
                        out = term if out is None else out + term
                        product = shifted * signal
                        folded = product[0:8]
                        for r in range(8, TILE, 8):
                            folded = folded + product[r : r + 8]
                        sums[b, j, :, lane] += folded
                    store[0, pl.ds(base, TILE), lane] = out.astype(bf16)
            return 0

        lax.fori_loop(0, BLK // TILE, body, 0)

    order = ([blocks - 2, blocks - 1] + list(range(blocks - 3, -1, -1))) if blocks > 1 else [0]
    conv(0)
    pl.semaphore_wait(barrier, groups + rings - 2)
    share(0, 0)
    lag = 3
    for t in range(1, blocks + lag + 2):
        if t < blocks:
            conv(t)
            share(0, t)
        if t == lag:
            teach_copy.wait()
        if 0 <= t - lag < blocks:
            normalize(t - lag)
            gram(t - lag)
        if 0 <= t - lag - 1 < blocks:
            combine(t - lag - 1)
        if 0 <= t - lag - 2 < blocks:
            l = t - lag - 2
            residue(l)
            if l in order[:2]:
                for copy in own_rows(l):
                    copy.start()
    ready = []
    for i, l in enumerate(order):
        relay(l)
        if i + 2 < blocks:
            for copy in own_rows(order[i + 2]):
                copy.start()
        landed(l)
        fresh = [] if i == 0 and blocks > 1 else ([blocks - 1, blocks - 2] if i == 1 else [l])
        for at in fresh:
            multiply(at)
            ready.append(at)
            if len(ready) > 1:
                done = ready.pop(0)
                finish(done)
                back(done)
    finish(ready[0])
    back(ready[0])

    for b in range(2):
        for j in range(taps):
            mine[b, j : j + 1] = jnp.sum(sums[b, j], axis=0, keepdims=True)
        mine[b, taps:] = jnp.zeros((8 - taps, width), f32)

    tap_copies = [
        pltpu.make_async_remote_copy(
            src_ref=mine, dst_ref=others.at[step], send_sem=tap_send.at[step], recv_sem=tap_recv.at[step],
            device_id=(lax.rem(ring + step, rings), me), device_id_type=MESH,
        )
        for step in range(1, rings)
    ]
    for copy in tap_copies:
        copy.start()
    for l in range(blocks):
        for copy in (*stage_one(l), *stage_two(l), *own_rows(l), *relays(l)):
            copy.wait_send()
        for kind in range(2):
            for k, to in enumerate((across, along, diagonal)):
                here = small.at[kind, me, l]
                push(here, here, small_send.at[kind, k, l], small_recv.at[kind, me, l], to).wait_send()
    summed = [mine[b] for b in range(2)]
    for step, copy in enumerate(tap_copies):
        copy.wait_recv()
        summed = [summed[b] + others[step + 1, b] for b in range(2)]
    gate_taps[...] = summed[0][:taps] * norm_factor
    value_taps[...] = summed[1][:taps] * norm_factor
    for copy in tap_copies:
        copy.wait_send()


def quad_call(gate_raw, value_raw, filter_gate, filter_value, teacher):
    length, width = gate_raw.shape[1:]
    rings = lax.axis_size("seq")
    taps = filter_gate.shape[0]
    stripe, blocks = length // 4, length // BLK
    triangle = BLK * (blocks * (blocks + 1) // 2)
    norm_factor = 1.0 / math.sqrt(rings * length)
    f32, bf16 = jnp.float32, jnp.bfloat16
    any_space = pl.BlockSpec(memory_space=pl.ANY)
    vmem = pl.BlockSpec(memory_space=pltpu.VMEM)
    dma = pltpu.SemaphoreType.DMA
    return pl.pallas_call(
        functools.partial(quad_kernel, rings, taps, norm_factor),
        out_shape=(
            pltpu.VMEM(gate_raw.shape, bf16),
            pltpu.VMEM(gate_raw.shape, bf16),
            jax.ShapeDtypeStruct((taps, width), f32),
            jax.ShapeDtypeStruct((taps, width), f32),
        ),
        in_specs=[any_space, any_space, vmem, vmem, any_space],
        out_specs=(vmem, vmem, vmem, vmem),
        scratch_shapes=[
            pltpu.VMEM((length + PAD, width), bf16),
            pltpu.VMEM((length + PAD, width), bf16),
            pltpu.VMEM((length + PAD, width), f32),
            pltpu.VMEM((length + PAD, width), f32),
            pltpu.VMEM((length, width), bf16),
            pltpu.VMEM((length, width), bf16),
            pltpu.VMEM((stripe, length), f32),
            pltpu.VMEM((BLK, width), bf16),
            pltpu.VMEM((2, BLK // 4, triangle), f32),
            pltpu.VMEM((2, BLK // 4, triangle), bf16),
            pltpu.VMEM((2, BLK // 4, triangle), bf16),
            pltpu.VMEM((2, BLK // 8, triangle), bf16),
            pltpu.VMEM((2, BLK // 8, triangle), bf16),
            pltpu.VMEM((length, length), bf16),
            pltpu.VMEM((2, BLK, width), f32),
            pltpu.VMEM((length + PAD, width), f32),
            pltpu.VMEM((BLK, 128), f32),
            pltpu.VMEM((2, 4, blocks, 8, BLK), f32),
            pltpu.VMEM((length, 128), f32),
            pltpu.VMEM((2, taps, 8, width), f32),
            pltpu.VMEM((2, 8, width), f32),
            pltpu.VMEM((rings, 2, 8, width), f32),
            dma((3, blocks)),
            dma((2, blocks)),
            dma((2, blocks)),
            dma((2, blocks)),
            dma((2, blocks)),
            dma((6, blocks)),
            dma((6, blocks)),
            dma((2, 3, blocks)),
            dma((2, 4, blocks)),
            dma((rings,)),
            dma((rings,)),
        ],
        compiler_params=pltpu.CompilerParams(
            collective_id=0, has_side_effects=True, vmem_limit_bytes=58 * 1024 * 1024
        ),
    )(gate_raw, value_raw, filter_gate, filter_value, teacher)


def stripe_call(gate_raw, value_raw, filter_gate, filter_value, teacher):
    seq_count, length, width = gate_raw.shape
    groups, rings = lax.axis_size("chan"), lax.axis_size("seq")
    taps = filter_gate.shape[0]
    stripe, full = length // groups, width * groups
    norm_factor = 1.0 / math.sqrt(rings * seq_count * length)
    f32, bf16 = jnp.float32, jnp.bfloat16
    any_space = pl.BlockSpec(memory_space=pl.ANY)
    vmem = pl.BlockSpec(memory_space=pltpu.VMEM)
    dma = pltpu.SemaphoreType.DMA
    return pl.pallas_call(
        functools.partial(stripe_kernel, groups, rings, taps, norm_factor),
        out_shape=(
            pltpu.VMEM(gate_raw.shape, bf16),
            pltpu.VMEM(gate_raw.shape, bf16),
            jax.ShapeDtypeStruct((taps, width), f32),
            jax.ShapeDtypeStruct((taps, width), f32),
        ),
        in_specs=[any_space, any_space, vmem, vmem, any_space],
        out_specs=(vmem, vmem, vmem, vmem),
        scratch_shapes=[
            pltpu.VMEM((length + PAD, width), bf16),
            pltpu.VMEM((length + PAD, width), bf16),
            pltpu.VMEM((length + PAD, width), f32),
            pltpu.VMEM((length + PAD, width), f32),
            pltpu.VMEM((groups + 1, length, width), bf16),
            pltpu.VMEM((stripe, length), f32),
            pltpu.VMEM((stripe, full), bf16),
            pltpu.VMEM((stripe, full), bf16),
            pltpu.VMEM((stripe, full), f32),
            pltpu.VMEM((groups, stripe, width), bf16),
            pltpu.VMEM((length + PAD, width), bf16),
            pltpu.VMEM((2, taps, 8, width), f32),
            pltpu.VMEM((2, 8, width), f32),
            pltpu.VMEM((rings, 2, 8, width), f32),
            dma((3, groups)),
            dma((groups, groups)),
            dma((groups, groups)),
            dma((groups, 4)),
            dma((groups, 4)),
            dma((rings,)),
            dma((rings,)),
        ],
        compiler_params=pltpu.CompilerParams(
            collective_id=0, has_side_effects=True, vmem_limit_bytes=52 * 1024 * 1024
        ),
    )(gate_raw, value_raw, filter_gate, filter_value, teacher)


def on_device(gate_raw, value_raw, filter_gate, filter_value, teacher):
    length, width = gate_raw.shape[1:]
    groups = lax.axis_size("chan")
    square = groups == 4 and gate_raw.shape[0] == 1 and (length // 4) % BLK == 0 and width % 128 == 0
    call = quad_call if square else stripe_call
    return call(gate_raw, value_raw, filter_gate, filter_value, teacher)


def solution(mesh):
    placed = (
        P("seq", None, "chan"),
        P("seq", None, "chan"),
        P(None, "chan"),
        P(None, "chan"),
        P("seq", "chan", None),
    )
    return jax.shard_map(
        on_device,
        mesh=mesh,
        in_specs=placed,
        out_specs=(
            P("seq", None, "chan"),
            P("seq", None, "chan"),
            P(None, "chan"),
            P(None, "chan"),
        ),
        check_vma=False,
    )
```

```python
import functools
import math

import jax
import jax.numpy as jnp
from jax import lax
from jax.experimental import pallas as pl
from jax.experimental.pallas import tpu as pltpu
from jax.sharding import PartitionSpec as P

epsilon = 1e-06
PAD = 16
TILE = 64
BLK = 256
MESH = pl.DeviceIdType.MESH


def stripe_kernel(
    groups, rings, taps, norm_factor,
    gate_in, value_in, filter_gate, filter_value, teacher_in,
    gate_out, value_out, gate_taps, value_taps,
    raw_g, raw_v, conv_g, conv_v, held, teach, own_n, block_n, total, outgoing, hgrad,
    sums, mine, others,
    in_sem, send_sem, recv_sem, a2a_send, a2a_recv, tap_send, tap_recv,
):
    length, width = gate_in.shape[1:]
    stripe = length // groups
    full = width * groups
    factor = 16.0 / math.sqrt(length)
    tile = min(TILE, stripe)
    lanes = [slice(k, min(k + 128, width)) for k in range(0, width, 128)]
    f32, bf16 = jnp.float32, jnp.bfloat16
    me, ring = lax.axis_index("chan"), lax.axis_index("seq")
    base_at, slot, proc = me, me, ring

    def rows_of(chunk, size=stripe, start=0):
        return pl.ds(pl.multiple_of(chunk * stripe + start, math.gcd(stripe, start) if start else stripe), size)

    in_copies = []
    for c in range(groups):
        span = pl.ds(c * stripe, stripe)
        dest = pl.ds(PAD + c * stripe, stripe)
        for k, (src, dst) in enumerate(((gate_in, raw_g), (value_in, raw_v))):
            in_copies.append(pltpu.make_async_copy(src.at[0, span], dst.at[dest], in_sem.at[k, c]))
    for copy in in_copies:
        copy.start()
    teach_copy = pltpu.make_async_copy(teacher_in.at[0], teach, in_sem.at[2, 0])
    teach_copy.start()

    barrier = pltpu.get_barrier_semaphore()
    for step in range(1, groups):
        pl.semaphore_signal(barrier, inc=1, device_id=(ring, lax.rem(me + step, groups)), device_id_type=MESH)
    greeted = groups + rings - 2
    for step in range(1, rings):
        pl.semaphore_signal(barrier, inc=1, device_id=(lax.rem(ring + step, rings), me), device_id_type=MESH)

    raw_g[0:PAD] = jnp.zeros((PAD, width), bf16)
    raw_v[0:PAD] = jnp.zeros((PAD, width), bf16)
    conv_g[length:] = jnp.zeros((PAD, width), f32)
    conv_v[length:] = jnp.zeros((PAD, width), f32)
    hgrad[length:] = jnp.zeros((PAD, width), bf16)
    sums[...] = jnp.zeros(sums.shape, f32)
    total[...] = jnp.zeros(total.shape, f32)
    for copy in in_copies:
        copy.wait()

    def conv_chunk(chunk):
        def body(i, _):
            base = pl.multiple_of(chunk * stripe + i * tile, tile)
            for lane in lanes:
                made = []
                for raw, weights, store in ((raw_g, filter_gate, conv_g), (raw_v, filter_value, conv_v)):
                    window = raw[pl.ds(base, tile + PAD), lane].astype(f32)
                    out = weights[0:1, lane] * window[PAD:]
                    for j in range(1, taps):
                        out = out + weights[j : j + 1, lane] * pltpu.roll(window, j, 0)[PAD:]
                    store[pl.ds(base, tile), lane] = out
                    made.append(out)
                held[slot, pl.ds(base, tile), lane] = (made[0] * made[1]).astype(bf16)
            return 0

        lax.fori_loop(0, stripe // tile, body, 0)

    def gather_copy(source, target, chunk, to, send):
        rows = rows_of(chunk)
        return pltpu.make_async_remote_copy(
            src_ref=held.at[source, rows], dst_ref=held.at[target, rows],
            send_sem=send, recv_sem=recv_sem.at[target, chunk],
            device_id=to, device_id_type=MESH,
        )

    def arrived(source, chunk):
        gather_copy(source, source, chunk, (ring, me), send_sem.at[0, 0]).wait_recv()

    for c in range(groups):
        conv_chunk(c)
    pl.semaphore_wait(barrier, greeted)

    def send_all(copy_do):
        def body(i, _):
            chunk, step = i // (groups - 1), 1 + lax.rem(i, groups - 1)
            copy_do(gather_copy(me, me, chunk, (ring, lax.rem(me + step, groups)), send_sem.at[step, chunk]))
            return 0

        lax.fori_loop(0, groups * (groups - 1), body, 0)

    send_all(lambda copy: copy.start())

    def wait_chunk(chunk):
        def body(step, _):
            arrived(lax.rem(me + step, groups), chunk)
            return 0

        lax.fori_loop(1, groups, body, 0)

    norm_tile = min(32, stripe)

    def scale_of(base):
        squares = jnp.zeros((norm_tile, width), f32)
        for g in range(groups):
            block = held[g, pl.ds(base, norm_tile)].astype(f32)
            squares = squares + block * block
        return lax.rsqrt(jnp.sum(squares, axis=1, keepdims=True) / full + epsilon)

    def normalize(chunk, dest):
        def body(i, _):
            base = pl.multiple_of(chunk * stripe + i * norm_tile, norm_tile)
            inverse = scale_of(base)
            for g in range(groups):
                block = held[g, pl.ds(base, norm_tile)].astype(f32)
                dest[pl.ds(pl.multiple_of(i * norm_tile, norm_tile), norm_tile), g * width : (g + 1) * width] = (
                    block * inverse
                ).astype(bf16)
            return 0

        lax.fori_loop(0, stripe // norm_tile, body, 0)

    teach_copy.wait()
    mat = min(256, stripe)

    def gram_chunk(t, _):
        chunk = lax.rem(me + t, groups)
        wait_chunk(chunk)
        normalize(chunk, block_n)

        @pl.when(t == 0)
        def _():
            own_n[...] = block_n[...]

        def body(m, _):
            rows = pl.ds(pl.multiple_of(m * mat, mat), mat)
            similarity = lax.dot_general(
                own_n[rows], block_n[...], (((1,), (1,)), ((), ())), preferred_element_type=f32
            ) / full
            residue = (factor * (similarity - teach[rows, rows_of(chunk)])).astype(bf16)
            total[rows] += jnp.dot(residue, block_n[...], preferred_element_type=f32)
            return 0

        lax.fori_loop(0, stripe // mat, body, 0)
        return 0

    lax.fori_loop(0, groups, gram_chunk, 0)

    def finish(i, _):
        local = pl.multiple_of(i * norm_tile, norm_tile)
        base = pl.multiple_of(base_at * stripe + i * norm_tile, norm_tile)
        rows = pl.ds(local, norm_tile)
        inverse = scale_of(base)
        inner = jnp.zeros((norm_tile, width), f32)
        for g in range(groups):
            part = slice(g * width, (g + 1) * width)
            inner = inner + held[g, pl.ds(base, norm_tile)].astype(f32) * inverse * total[rows, part]
        projection = jnp.sum(inner, axis=1, keepdims=True) / full
        for g in range(groups):
            part = slice(g * width, (g + 1) * width)
            normed = held[g, pl.ds(base, norm_tile)].astype(f32) * inverse
            outgoing[g, rows] = (inverse * (total[rows, part] - normed * projection)).astype(bf16)
        return 0

    pieces = max(1, min(4, stripe // 128))
    piece = stripe // pieces
    steps = piece // norm_tile

    def exchange(target, p, source_row):
        return pltpu.make_async_remote_copy(
            src_ref=outgoing.at[target, pl.ds(p * piece, piece)],
            dst_ref=hgrad.at[rows_of(source_row, piece, p * piece)],
            send_sem=a2a_send.at[target, p], recv_sem=a2a_recv.at[source_row, p],
            device_id=(proc, target), device_id_type=MESH,
        )

    targets = tuple(lax.rem(me + groups - step, groups) for step in range(1, groups))

    def stay(p):
        hgrad[rows_of(base_at, piece, p * piece)] = outgoing[me, pl.ds(p * piece, piece)]

    for p in reversed(range(pieces)):
        lax.fori_loop(p * steps, (p + 1) * steps, finish, 0)
        for target in targets:
            exchange(target, p, base_at).start()
        stay(p)

    def back_tile(base):
        for k in range(0, width, 128):
            lane = slice(k, min(k + 128, width))
            up = hgrad[pl.ds(base, tile + PAD), lane].astype(f32)
            for b, (conv, raw, weights, store) in enumerate(
                ((conv_v, raw_g, filter_gate, gate_out), (conv_g, raw_v, filter_value, value_out))
            ):
                window = up * conv[pl.ds(base, tile + PAD), lane]
                signal = raw[pl.ds(pl.multiple_of(base + PAD, PAD), tile), lane].astype(f32)
                out = None
                for j in range(taps):
                    shifted = (window if j == 0 else pltpu.roll(window, tile + PAD - j, 0))[:tile]
                    term = weights[j : j + 1, lane] * shifted
                    out = term if out is None else out + term
                    product = shifted * signal
                    folded = product[0:8]
                    for r in range(8, tile, 8):
                        folded = folded + product[r : r + 8]
                    sums[b, j, :, lane] += folded
                store[0, pl.ds(base, tile), lane] = out.astype(bf16)

    tiles = stripe // tile
    per = tiles // pieces
    sources = tuple(lax.rem(me + step, groups) for step in range(groups))
    for p in reversed(range(pieces)):
        for step, source in enumerate(sources):
            def landed(p=p, source=source):
                exchange(source, p, source).wait_recv()

            if step:
                landed()

            def inner_tiles(i, _, source=source):
                back_tile(pl.multiple_of(source * stripe + i * tile, tile))
                return 0

            lax.fori_loop(p * per, (p + 1) * per - (1 if p == pieces - 1 else 0), inner_tiles, 0)

    def last_tiles(c, _):
        back_tile(pl.multiple_of(c * stripe + (tiles - 1) * tile, tile))
        return 0

    lax.fori_loop(0, groups, last_tiles, 0)
    for b in range(2):
        for j in range(taps):
            mine[b, j : j + 1] = jnp.sum(sums[b, j], axis=0, keepdims=True)
        mine[b, taps:] = jnp.zeros((8 - taps, width), f32)

    def tap_copy(to, slot):
        return pltpu.make_async_remote_copy(
            src_ref=mine, dst_ref=others.at[slot], send_sem=tap_send.at[slot], recv_sem=tap_recv.at[slot],
            device_id=(to, me), device_id_type=MESH,
        )

    tap_copies = [tap_copy(lax.rem(ring + step, rings), step) for step in range(1, rings)]
    for copy in tap_copies:
        copy.start()
    summed = [mine[b] for b in range(2)]
    for step, copy in enumerate(tap_copies):
        copy.wait_recv()
        summed = [summed[b] + others[step + 1, b] for b in range(2)]
    gate_taps[...] = summed[0][:taps] * norm_factor
    value_taps[...] = summed[1][:taps] * norm_factor

    for copy in tap_copies:
        copy.wait_send()
    send_all(lambda copy: copy.wait_send())
    for target in targets:
        for p in range(pieces):
            exchange(target, p, base_at).wait_send()


def quad_kernel(
    rings, taps, norm_factor,
    gate_in, value_in, filter_gate, filter_value, teacher_in,
    gate_out, value_out, gate_taps, value_taps,
    raw_g, raw_v, conv_g, conv_v, hid, nrm, teach, perm, keep,
    s1, r1, s2, r2, res, gbuf, hgrad, lane_sums, small, invc,
    sums, mine, others,
    in_sem, s1_send, s1_recv, s2_send, s2_recv, ag_send, ag_recv,
    small_send, small_recv, tap_send, tap_recv,
):
    groups = 4
    length, width = gate_in.shape[1:]
    stripe, full = length // groups, width * groups
    factor = 16.0 / math.sqrt(length)
    blocks = length // BLK
    half, quarter, eighth = BLK // 2, BLK // 4, BLK // 8
    lanes = [slice(k, k + 128) for k in range(0, width, 128)]
    f32, bf16 = jnp.float32, jnp.bfloat16
    me, ring = lax.axis_index("chan"), lax.axis_index("seq")
    x, y = lax.rem(me, 2), me // 2
    across, along, diagonal = me + 1 - 2 * x, lax.rem(me + 2, 4), 3 - me
    offset = [BLK * (l * (l + 1) // 2) for l in range(blocks)]

    def rows(start, size, unit=None):
        return pl.ds(pl.multiple_of(start, unit or size), size)

    def push(src, dst, send, recv, to):
        return pltpu.make_async_remote_copy(
            src_ref=src, dst_ref=dst, send_sem=send, recv_sem=recv,
            device_id=(ring, to), device_id_type=MESH,
        )

    in_copies = []
    for l in range(blocks):
        for k, (src, dst) in enumerate(((gate_in, raw_g), (value_in, raw_v))):
            in_copies.append(pltpu.make_async_copy(
                src.at[0, pl.ds(l * BLK, BLK)], dst.at[pl.ds(PAD + l * BLK, BLK)], in_sem.at[k, l]
            ))
    for copy in in_copies:
        copy.start()
    teach_copy = pltpu.make_async_copy(teacher_in.at[0], teach, in_sem.at[2, 0])
    teach_copy.start()

    barrier = pltpu.get_barrier_semaphore()
    for to in (across, along, diagonal):
        pl.semaphore_signal(barrier, inc=1, device_id=(ring, to), device_id_type=MESH)
    for step in range(1, rings):
        pl.semaphore_signal(barrier, inc=1, device_id=(lax.rem(ring + step, rings), me), device_id_type=MESH)

    raw_g[0:PAD] = jnp.zeros((PAD, width), bf16)
    raw_v[0:PAD] = jnp.zeros((PAD, width), bf16)
    conv_g[length:] = jnp.zeros((PAD, width), f32)
    conv_v[length:] = jnp.zeros((PAD, width), f32)
    hgrad[length:] = jnp.zeros((PAD, width), f32)
    sums[...] = jnp.zeros(sums.shape, f32)

    def share(kind, l):
        small[kind, me, l] = jnp.broadcast_to(jnp.sum(lane_sums[...].T, axis=0, keepdims=True), (8, BLK))
        for k, to in enumerate((across, along, diagonal)):
            here = small.at[kind, me, l]
            push(here, here, small_send.at[kind, k, l], small_recv.at[kind, me, l], to).start()

    def total(kind, l):
        for o in (across, along, diagonal):
            there = small.at[kind, o, l]
            push(there, there, small_send.at[kind, 0, l], small_recv.at[kind, o, l], o).wait_recv()
        return small[kind, 0, l, 0:1] + small[kind, 1, l, 0:1] + small[kind, 2, l, 0:1] + small[kind, 3, l, 0:1]

    def column(row):
        return jnp.broadcast_to(row, (128, BLK)).T

    def conv(l):
        in_copies[2 * l].wait()
        in_copies[2 * l + 1].wait()

        def body(i, _):
            base = pl.multiple_of(l * BLK + i * TILE, TILE)
            squares = jnp.zeros((TILE, 128), f32)
            for lane in lanes:
                made = []
                for raw, weights, store in ((raw_g, filter_gate, conv_g), (raw_v, filter_value, conv_v)):
                    window = raw[pl.ds(base, TILE + PAD), lane].astype(f32)
                    out = weights[0:1, lane] * window[PAD:]
                    for j in range(1, taps):
                        out = out + weights[j : j + 1, lane] * pltpu.roll(window, j, 0)[PAD:]
                    store[pl.ds(base, TILE), lane] = out
                    made.append(out)
                hidden = (made[0] * made[1]).astype(bf16)
                hid[pl.ds(base, TILE), lane] = hidden
                hidden = hidden.astype(f32)
                squares = squares + hidden * hidden
            lane_sums[pl.ds(pl.multiple_of(i * TILE, TILE), TILE)] = squares
            return 0

        lax.fori_loop(0, BLK // TILE, body, 0)

    def normalize(l):
        invc[pl.ds(l * BLK, BLK)] = column(lax.rsqrt(total(0, l) / full + epsilon))

        def body(i, _):
            base = pl.multiple_of(l * BLK + i * TILE, TILE)
            inverse = invc[pl.ds(base, TILE)]
            for lane in lanes:
                nrm[pl.ds(base, TILE), lane] = (hid[pl.ds(base, TILE), lane].astype(f32) * inverse).astype(bf16)
            return 0

        lax.fori_loop(0, BLK // TILE, body, 0)

    pieces = (quarter * (1 - x), half + quarter * (1 - y), quarter * x, half + quarter * y)

    def reach(l, k):
        return l * BLK + (half if k == 0 else BLK)

    def stage_one(l):
        for k, to in enumerate((across, along)):
            span = pl.ds(offset[l], reach(l, k))
            yield push(s1.at[k, :, span], r1.at[k, :, span], s1_send.at[k, l], s1_recv.at[k, l], to)

    def stage_two(l):
        for k, to in enumerate((across, along)):
            span = pl.ds(offset[l], reach(l, 1 - k))
            yield push(s2.at[k, :, span], r2.at[k, :, span], s2_send.at[k, l], s2_recv.at[k, l], to)

    def gram(l):
        for k, piece in enumerate(pieces):
            perm[k * quarter : (k + 1) * quarter] = nrm[rows(l * BLK + piece, quarter)]
        top = (l * BLK) % stripe
        held = jnp.where(me == (l * BLK) // stripe, 1.0, 0.0)

        def body(j, _):
            part = lax.dot_general(
                perm[...], nrm[rows(j * BLK, BLK)], (((1,), (1,)), ((), ())), preferred_element_type=f32
            ) / full
            cols = rows(offset[l] + j * BLK, BLK)
            for k, piece in enumerate(pieces):
                target = teach[rows(top + piece, quarter), rows(j * BLK, BLK)]
                apart = part[k * quarter : (k + 1) * quarter] - held * target
                if k < 2:
                    s1[k, :, cols] = apart.astype(bf16)
                else:
                    keep[k - 2, :, cols] = apart
            return 0

        lax.fori_loop(0, l + 1, body, 0)
        for copy in stage_one(l):
            copy.start()

    turns = ((0, y), (1, x))

    def combine(l):
        for copy in stage_one(l):
            copy.wait_recv()

        def add(k, own, cols):
            away = rows(eighth * (1 - own), eighth)
            s2[1 - k, :, cols] = (keep[k, away, cols] + r1[k, away, cols].astype(f32)).astype(bf16)

        def body(j, _):
            for k, own in turns:
                add(k, own, rows(offset[l] + j * BLK, BLK))
            return 0

        lax.fori_loop(0, l, body, 0)
        for k, own in turns:
            add(k, own, pl.ds(offset[l] + l * BLK, half if k == 0 else BLK))
        for copy in stage_two(l):
            copy.start()

    def place(l, k, px, py):
        return l * BLK + (quarter * px + eighth * py if k == 0 else half + quarter * py + eighth * px)

    def residue(l):
        for copy in stage_two(l):
            copy.wait_recv()

        def add(k, own, cols, dest):
            here = rows(eighth * own, eighth)
            apart = keep[k, here, cols] + r1[k, here, cols].astype(f32) + r2[1 - k, :, cols].astype(f32)
            res[rows(place(l, k, x, y), eighth), dest] = (factor * apart).astype(bf16)

        def body(j, _):
            for k, own in turns:
                add(k, own, rows(offset[l] + j * BLK, BLK), rows(j * BLK, BLK))
            return 0

        lax.fori_loop(0, l, body, 0)
        for k, own in turns:
            size = half if k == 0 else BLK
            add(k, own, pl.ds(offset[l] + l * BLK, size), pl.ds(l * BLK, size))

    def gather(l, slot, k, px, py, to):
        area = res.at[rows(place(l, k, px, py), eighth), pl.ds(0, reach(l, k))]
        return push(area, area, ag_send.at[slot, l], ag_recv.at[slot, l], to)

    def own_rows(l):
        return (
            gather(l, 0, 0, x, y, across), gather(l, 3, 1, x, y, along),
            gather(l, 1, 1, x, y, across), gather(l, 2, 0, x, y, along),
        )

    def relays(l):
        return gather(l, 4, 0, 1 - x, y, along), gather(l, 5, 1, x, 1 - y, across)

    def relay(l):
        first, second = relays(l)
        gather(l, 0, 0, 1 - x, y, across).wait_recv()
        first.start()
        gather(l, 3, 1, x, 1 - y, along).wait_recv()
        second.start()

    def landed(l):
        gather(l, 1, 1, 1 - x, y, across).wait_recv()
        gather(l, 2, 0, x, 1 - y, along).wait_recv()
        gather(l, 4, 0, 1 - x, 1 - y, along).wait_recv()
        gather(l, 5, 1, 1 - x, 1 - y, across).wait_recv()

    def multiply(l):
        start, stop, mid = l * BLK, (l + 1) * BLK, l * BLK + half
        res[start:mid, mid:stop] = res[mid:stop, start:mid].T
        out = jnp.dot(res[start:stop, 0:stop], nrm[0:stop], preferred_element_type=f32)
        if stop < length:
            out = out + lax.dot_general(
                res[stop:length, start:stop], nrm[stop:length], (((0,), (0,)), ((), ())), preferred_element_type=f32
            )
        gbuf[l % 3] = out

        def body(i, _):
            local = rows(i * TILE, TILE)
            at = rows(start + i * TILE, TILE)
            inner = jnp.zeros((TILE, 128), f32)
            for lane in lanes:
                inner = inner + hid[at, lane].astype(f32) * invc[at] * gbuf[l % 3, local, lane]
            lane_sums[local] = inner
            return 0

        lax.fori_loop(0, BLK // TILE, body, 0)
        share(1, l)

    def finish(l):
        lane_sums[...] = column(total(1, l) / full)

        def body(i, _):
            local = rows(i * TILE, TILE)
            at = rows(l * BLK + i * TILE, TILE)
            inverse, projection = invc[at], lane_sums[local]
            for lane in lanes:
                normed = hid[at, lane].astype(f32) * inverse
                hgrad[at, lane] = inverse * (gbuf[l % 3, local, lane] - normed * projection)
            return 0

        lax.fori_loop(0, BLK // TILE, body, 0)

    def back(l):
        def body(i, _):
            base = pl.multiple_of(l * BLK + i * TILE, TILE)
            for lane in lanes:
                up = hgrad[pl.ds(base, TILE + PAD), lane]
                for b, (conv_by, raw, weights, store) in enumerate(
                    ((conv_v, raw_g, filter_gate, gate_out), (conv_g, raw_v, filter_value, value_out))
                ):
                    window = up * conv_by[pl.ds(base, TILE + PAD), lane]
                    signal = raw[pl.ds(pl.multiple_of(base + PAD, PAD), TILE), lane].astype(f32)
                    out = None
                    for j in range(taps):
                        shifted = (window if j == 0 else pltpu.roll(window, TILE + PAD - j, 0))[:TILE]
                        term = weights[j : j + 1, lane] * shifted
                        out = term if out is None else out + term
                        product = shifted * signal
                        folded = product[0:8]
                        for r in range(8, TILE, 8):
                            folded = folded + product[r : r + 8]
                        sums[b, j, :, lane] += folded
                    store[0, pl.ds(base, TILE), lane] = out.astype(bf16)
            return 0

        lax.fori_loop(0, BLK // TILE, body, 0)

    order = ([blocks - 2, blocks - 1] + list(range(blocks - 3, -1, -1))) if blocks > 1 else [0]
    begin, hop = 2, 2
    for t in range(blocks + begin + 2 * hop):
        if t < blocks:
            conv(t)
            if t == 0:
                pl.semaphore_wait(barrier, groups + rings - 2)
            share(0, t)
        l = t - begin
        if l == 0:
            teach_copy.wait()
        if 0 <= l < blocks:
            normalize(l)
            gram(l)
        l = l - hop
        if 0 <= l < blocks:
            combine(l)
        l = l - hop
        if 0 <= l < blocks:
            residue(l)
            if l in order[:2]:
                for copy in own_rows(l):
                    copy.start()

    def send_own(i):
        if i < blocks:
            for copy in own_rows(order[i]):
                copy.start()

    relay(order[0])
    send_own(2)
    ready = []
    for i, l in enumerate(order):
        landed(l)
        if i + 1 < blocks:
            relay(order[i + 1])
        send_own(i + 3)
        for at in [] if i == 0 and blocks > 1 else ([blocks - 1, blocks - 2] if i == 1 else [l]):
            multiply(at)
            ready.append(at)
            if len(ready) > 2:
                done = ready.pop(0)
                finish(done)
                back(done)
    for done in ready:
        finish(done)
        back(done)

    for b in range(2):
        for j in range(taps):
            mine[b, j : j + 1] = jnp.sum(sums[b, j], axis=0, keepdims=True)
        mine[b, taps:] = jnp.zeros((8 - taps, width), f32)

    tap_copies = [
        pltpu.make_async_remote_copy(
            src_ref=mine, dst_ref=others.at[step], send_sem=tap_send.at[step], recv_sem=tap_recv.at[step],
            device_id=(lax.rem(ring + step, rings), me), device_id_type=MESH,
        )
        for step in range(1, rings)
    ]
    for copy in tap_copies:
        copy.start()
    for l in range(blocks):
        for copy in (*stage_one(l), *stage_two(l), *own_rows(l), *relays(l)):
            copy.wait_send()
        for kind in range(2):
            for k, to in enumerate((across, along, diagonal)):
                here = small.at[kind, me, l]
                push(here, here, small_send.at[kind, k, l], small_recv.at[kind, me, l], to).wait_send()
    summed = [mine[b] for b in range(2)]
    for step, copy in enumerate(tap_copies):
        copy.wait_recv()
        summed = [summed[b] + others[step + 1, b] for b in range(2)]
    gate_taps[...] = summed[0][:taps] * norm_factor
    value_taps[...] = summed[1][:taps] * norm_factor
    for copy in tap_copies:
        copy.wait_send()


def quad_call(gate_raw, value_raw, filter_gate, filter_value, teacher):
    length, width = gate_raw.shape[1:]
    rings = lax.axis_size("seq")
    taps = filter_gate.shape[0]
    stripe, blocks = length // 4, length // BLK
    triangle = BLK * (blocks * (blocks + 1) // 2)
    norm_factor = 1.0 / math.sqrt(rings * length)
    f32, bf16 = jnp.float32, jnp.bfloat16
    any_space = pl.BlockSpec(memory_space=pl.ANY)
    vmem = pl.BlockSpec(memory_space=pltpu.VMEM)
    dma = pltpu.SemaphoreType.DMA
    return pl.pallas_call(
        functools.partial(quad_kernel, rings, taps, norm_factor),
        out_shape=(
            pltpu.VMEM(gate_raw.shape, bf16),
            pltpu.VMEM(gate_raw.shape, bf16),
            jax.ShapeDtypeStruct((taps, width), f32),
            jax.ShapeDtypeStruct((taps, width), f32),
        ),
        in_specs=[any_space, any_space, vmem, vmem, any_space],
        out_specs=(vmem, vmem, vmem, vmem),
        scratch_shapes=[
            pltpu.VMEM((length + PAD, width), bf16),
            pltpu.VMEM((length + PAD, width), bf16),
            pltpu.VMEM((length + PAD, width), f32),
            pltpu.VMEM((length + PAD, width), f32),
            pltpu.VMEM((length, width), bf16),
            pltpu.VMEM((length, width), bf16),
            pltpu.VMEM((stripe, length), f32),
            pltpu.VMEM((BLK, width), bf16),
            pltpu.VMEM((2, BLK // 4, triangle), f32),
            pltpu.VMEM((2, BLK // 4, triangle), bf16),
            pltpu.VMEM((2, BLK // 4, triangle), bf16),
            pltpu.VMEM((2, BLK // 8, triangle), bf16),
            pltpu.VMEM((2, BLK // 8, triangle), bf16),
            pltpu.VMEM((length, length), bf16),
            pltpu.VMEM((3, BLK, width), f32),
            pltpu.VMEM((length + PAD, width), f32),
            pltpu.VMEM((BLK, 128), f32),
            pltpu.VMEM((2, 4, blocks, 8, BLK), f32),
            pltpu.VMEM((length, 128), f32),
            pltpu.VMEM((2, taps, 8, width), f32),
            pltpu.VMEM((2, 8, width), f32),
            pltpu.VMEM((rings, 2, 8, width), f32),
            dma((3, blocks)),
            dma((2, blocks)),
            dma((2, blocks)),
            dma((2, blocks)),
            dma((2, blocks)),
            dma((6, blocks)),
            dma((6, blocks)),
            dma((2, 3, blocks)),
            dma((2, 4, blocks)),
            dma((rings,)),
            dma((rings,)),
        ],
        compiler_params=pltpu.CompilerParams(
            collective_id=0, has_side_effects=True, vmem_limit_bytes=58 * 1024 * 1024
        ),
    )(gate_raw, value_raw, filter_gate, filter_value, teacher)


def stripe_call(gate_raw, value_raw, filter_gate, filter_value, teacher):
    seq_count, length, width = gate_raw.shape
    groups, rings = lax.axis_size("chan"), lax.axis_size("seq")
    taps = filter_gate.shape[0]
    stripe, full = length // groups, width * groups
    norm_factor = 1.0 / math.sqrt(rings * seq_count * length)
    f32, bf16 = jnp.float32, jnp.bfloat16
    any_space = pl.BlockSpec(memory_space=pl.ANY)
    vmem = pl.BlockSpec(memory_space=pltpu.VMEM)
    dma = pltpu.SemaphoreType.DMA
    return pl.pallas_call(
        functools.partial(stripe_kernel, groups, rings, taps, norm_factor),
        out_shape=(
            pltpu.VMEM(gate_raw.shape, bf16),
            pltpu.VMEM(gate_raw.shape, bf16),
            jax.ShapeDtypeStruct((taps, width), f32),
            jax.ShapeDtypeStruct((taps, width), f32),
        ),
        in_specs=[any_space, any_space, vmem, vmem, any_space],
        out_specs=(vmem, vmem, vmem, vmem),
        scratch_shapes=[
            pltpu.VMEM((length + PAD, width), bf16),
            pltpu.VMEM((length + PAD, width), bf16),
            pltpu.VMEM((length + PAD, width), f32),
            pltpu.VMEM((length + PAD, width), f32),
            pltpu.VMEM((groups + 1, length, width), bf16),
            pltpu.VMEM((stripe, length), f32),
            pltpu.VMEM((stripe, full), bf16),
            pltpu.VMEM((stripe, full), bf16),
            pltpu.VMEM((stripe, full), f32),
            pltpu.VMEM((groups, stripe, width), bf16),
            pltpu.VMEM((length + PAD, width), bf16),
            pltpu.VMEM((2, taps, 8, width), f32),
            pltpu.VMEM((2, 8, width), f32),
            pltpu.VMEM((rings, 2, 8, width), f32),
            dma((3, groups)),
            dma((groups, groups)),
            dma((groups, groups)),
            dma((groups, 4)),
            dma((groups, 4)),
            dma((rings,)),
            dma((rings,)),
        ],
        compiler_params=pltpu.CompilerParams(
            collective_id=0, has_side_effects=True, vmem_limit_bytes=52 * 1024 * 1024
        ),
    )(gate_raw, value_raw, filter_gate, filter_value, teacher)


def on_device(gate_raw, value_raw, filter_gate, filter_value, teacher):
    length, width = gate_raw.shape[1:]
    groups = lax.axis_size("chan")
    square = groups == 4 and gate_raw.shape[0] == 1 and (length // 4) % BLK == 0 and width % 128 == 0
    call = quad_call if square else stripe_call
    return call(gate_raw, value_raw, filter_gate, filter_value, teacher)


def solution(mesh):
    placed = (
        P("seq", None, "chan"),
        P("seq", None, "chan"),
        P(None, "chan"),
        P(None, "chan"),
        P("seq", "chan", None),
    )
    return jax.shard_map(
        on_device,
        mesh=mesh,
        in_specs=placed,
        out_specs=(
            P("seq", None, "chan"),
            P("seq", None, "chan"),
            P(None, "chan"),
            P(None, "chan"),
        ),
        check_vma=False,
    )
```

```python
import functools
import math

import jax
import jax.numpy as jnp
from jax import lax
from jax.experimental import pallas as pl
from jax.experimental.pallas import tpu as pltpu
from jax.sharding import PartitionSpec as P

epsilon = 1e-06
PAD = 16
TILE = 64
BLK = 256
EARLY = 0
LAG = 2
SPLIT = True
MESH = pl.DeviceIdType.MESH


def stripe_kernel(
    groups, rings, taps, norm_factor,
    gate_in, value_in, filter_gate, filter_value, teacher_in,
    gate_out, value_out, gate_taps, value_taps,
    raw_g, raw_v, conv_g, conv_v, held, teach, own_n, block_n, total, outgoing, hgrad,
    sums, mine, others,
    in_sem, send_sem, recv_sem, a2a_send, a2a_recv, tap_send, tap_recv,
):
    length, width = gate_in.shape[1:]
    stripe = length // groups
    full = width * groups
    factor = 16.0 / math.sqrt(length)
    tile = min(TILE, stripe)
    lanes = [slice(k, min(k + 128, width)) for k in range(0, width, 128)]
    f32, bf16 = jnp.float32, jnp.bfloat16
    me, ring = lax.axis_index("chan"), lax.axis_index("seq")
    base_at, slot, proc = me, me, ring

    def rows_of(chunk, size=stripe, start=0):
        return pl.ds(pl.multiple_of(chunk * stripe + start, math.gcd(stripe, start) if start else stripe), size)

    in_copies = []
    for c in range(groups):
        span = pl.ds(c * stripe, stripe)
        dest = pl.ds(PAD + c * stripe, stripe)
        for k, (src, dst) in enumerate(((gate_in, raw_g), (value_in, raw_v))):
            in_copies.append(pltpu.make_async_copy(src.at[0, span], dst.at[dest], in_sem.at[k, c]))
    for copy in in_copies:
        copy.start()
    teach_copy = pltpu.make_async_copy(teacher_in.at[0], teach, in_sem.at[2, 0])
    teach_copy.start()

    barrier = pltpu.get_barrier_semaphore()
    for step in range(1, groups):
        pl.semaphore_signal(barrier, inc=1, device_id=(ring, lax.rem(me + step, groups)), device_id_type=MESH)
    greeted = groups + rings - 2
    for step in range(1, rings):
        pl.semaphore_signal(barrier, inc=1, device_id=(lax.rem(ring + step, rings), me), device_id_type=MESH)

    raw_g[0:PAD] = jnp.zeros((PAD, width), bf16)
    raw_v[0:PAD] = jnp.zeros((PAD, width), bf16)
    conv_g[length:] = jnp.zeros((PAD, width), f32)
    conv_v[length:] = jnp.zeros((PAD, width), f32)
    hgrad[length:] = jnp.zeros((PAD, width), bf16)
    sums[...] = jnp.zeros(sums.shape, f32)
    total[...] = jnp.zeros(total.shape, f32)
    for copy in in_copies:
        copy.wait()

    def conv_chunk(chunk):
        def body(i, _):
            base = pl.multiple_of(chunk * stripe + i * tile, tile)
            for lane in lanes:
                made = []
                for raw, weights, store in ((raw_g, filter_gate, conv_g), (raw_v, filter_value, conv_v)):
                    window = raw[pl.ds(base, tile + PAD), lane].astype(f32)
                    out = weights[0:1, lane] * window[PAD:]
                    for j in range(1, taps):
                        out = out + weights[j : j + 1, lane] * pltpu.roll(window, j, 0)[PAD:]
                    store[pl.ds(base, tile), lane] = out
                    made.append(out)
                held[slot, pl.ds(base, tile), lane] = (made[0] * made[1]).astype(bf16)
            return 0

        lax.fori_loop(0, stripe // tile, body, 0)

    def gather_copy(source, target, chunk, to, send):
        rows = rows_of(chunk)
        return pltpu.make_async_remote_copy(
            src_ref=held.at[source, rows], dst_ref=held.at[target, rows],
            send_sem=send, recv_sem=recv_sem.at[target, chunk],
            device_id=to, device_id_type=MESH,
        )

    def arrived(source, chunk):
        gather_copy(source, source, chunk, (ring, me), send_sem.at[0, 0]).wait_recv()

    for c in range(groups):
        conv_chunk(c)
    pl.semaphore_wait(barrier, greeted)

    def send_all(copy_do):
        def body(i, _):
            chunk, step = i // (groups - 1), 1 + lax.rem(i, groups - 1)
            copy_do(gather_copy(me, me, chunk, (ring, lax.rem(me + step, groups)), send_sem.at[step, chunk]))
            return 0

        lax.fori_loop(0, groups * (groups - 1), body, 0)

    send_all(lambda copy: copy.start())

    def wait_chunk(chunk):
        def body(step, _):
            arrived(lax.rem(me + step, groups), chunk)
            return 0

        lax.fori_loop(1, groups, body, 0)

    norm_tile = min(32, stripe)

    def scale_of(base):
        squares = jnp.zeros((norm_tile, width), f32)
        for g in range(groups):
            block = held[g, pl.ds(base, norm_tile)].astype(f32)
            squares = squares + block * block
        return lax.rsqrt(jnp.sum(squares, axis=1, keepdims=True) / full + epsilon)

    def normalize(chunk, dest):
        def body(i, _):
            base = pl.multiple_of(chunk * stripe + i * norm_tile, norm_tile)
            inverse = scale_of(base)
            for g in range(groups):
                block = held[g, pl.ds(base, norm_tile)].astype(f32)
                dest[pl.ds(pl.multiple_of(i * norm_tile, norm_tile), norm_tile), g * width : (g + 1) * width] = (
                    block * inverse
                ).astype(bf16)
            return 0

        lax.fori_loop(0, stripe // norm_tile, body, 0)

    teach_copy.wait()
    mat = min(256, stripe)

    def gram_chunk(t, _):
        chunk = lax.rem(me + t, groups)
        wait_chunk(chunk)
        normalize(chunk, block_n)

        @pl.when(t == 0)
        def _():
            own_n[...] = block_n[...]

        def body(m, _):
            rows = pl.ds(pl.multiple_of(m * mat, mat), mat)
            similarity = lax.dot_general(
                own_n[rows], block_n[...], (((1,), (1,)), ((), ())), preferred_element_type=f32
            ) / full
            residue = (factor * (similarity - teach[rows, rows_of(chunk)])).astype(bf16)
            total[rows] += jnp.dot(residue, block_n[...], preferred_element_type=f32)
            return 0

        lax.fori_loop(0, stripe // mat, body, 0)
        return 0

    lax.fori_loop(0, groups, gram_chunk, 0)

    def finish(i, _):
        local = pl.multiple_of(i * norm_tile, norm_tile)
        base = pl.multiple_of(base_at * stripe + i * norm_tile, norm_tile)
        rows = pl.ds(local, norm_tile)
        inverse = scale_of(base)
        inner = jnp.zeros((norm_tile, width), f32)
        for g in range(groups):
            part = slice(g * width, (g + 1) * width)
            inner = inner + held[g, pl.ds(base, norm_tile)].astype(f32) * inverse * total[rows, part]
        projection = jnp.sum(inner, axis=1, keepdims=True) / full
        for g in range(groups):
            part = slice(g * width, (g + 1) * width)
            normed = held[g, pl.ds(base, norm_tile)].astype(f32) * inverse
            outgoing[g, rows] = (inverse * (total[rows, part] - normed * projection)).astype(bf16)
        return 0

    pieces = max(1, min(4, stripe // 128))
    piece = stripe // pieces
    steps = piece // norm_tile

    def exchange(target, p, source_row):
        return pltpu.make_async_remote_copy(
            src_ref=outgoing.at[target, pl.ds(p * piece, piece)],
            dst_ref=hgrad.at[rows_of(source_row, piece, p * piece)],
            send_sem=a2a_send.at[target, p], recv_sem=a2a_recv.at[source_row, p],
            device_id=(proc, target), device_id_type=MESH,
        )

    targets = tuple(lax.rem(me + groups - step, groups) for step in range(1, groups))

    def stay(p):
        hgrad[rows_of(base_at, piece, p * piece)] = outgoing[me, pl.ds(p * piece, piece)]

    for p in reversed(range(pieces)):
        lax.fori_loop(p * steps, (p + 1) * steps, finish, 0)
        for target in targets:
            exchange(target, p, base_at).start()
        stay(p)

    def back_tile(base):
        for k in range(0, width, 128):
            lane = slice(k, min(k + 128, width))
            up = hgrad[pl.ds(base, tile + PAD), lane].astype(f32)
            for b, (conv, raw, weights, store) in enumerate(
                ((conv_v, raw_g, filter_gate, gate_out), (conv_g, raw_v, filter_value, value_out))
            ):
                window = up * conv[pl.ds(base, tile + PAD), lane]
                signal = raw[pl.ds(pl.multiple_of(base + PAD, PAD), tile), lane].astype(f32)
                out = None
                for j in range(taps):
                    shifted = (window if j == 0 else pltpu.roll(window, tile + PAD - j, 0))[:tile]
                    term = weights[j : j + 1, lane] * shifted
                    out = term if out is None else out + term
                    product = shifted * signal
                    folded = product[0:8]
                    for r in range(8, tile, 8):
                        folded = folded + product[r : r + 8]
                    sums[b, j, :, lane] += folded
                store[0, pl.ds(base, tile), lane] = out.astype(bf16)

    tiles = stripe // tile
    per = tiles // pieces
    sources = tuple(lax.rem(me + step, groups) for step in range(groups))
    for p in reversed(range(pieces)):
        for step, source in enumerate(sources):
            def landed(p=p, source=source):
                exchange(source, p, source).wait_recv()

            if step:
                landed()

            def inner_tiles(i, _, source=source):
                back_tile(pl.multiple_of(source * stripe + i * tile, tile))
                return 0

            lax.fori_loop(p * per, (p + 1) * per - (1 if p == pieces - 1 else 0), inner_tiles, 0)

    def last_tiles(c, _):
        back_tile(pl.multiple_of(c * stripe + (tiles - 1) * tile, tile))
        return 0

    lax.fori_loop(0, groups, last_tiles, 0)
    for b in range(2):
        for j in range(taps):
            mine[b, j : j + 1] = jnp.sum(sums[b, j], axis=0, keepdims=True)
        mine[b, taps:] = jnp.zeros((8 - taps, width), f32)

    def tap_copy(to, slot):
        return pltpu.make_async_remote_copy(
            src_ref=mine, dst_ref=others.at[slot], send_sem=tap_send.at[slot], recv_sem=tap_recv.at[slot],
            device_id=(to, me), device_id_type=MESH,
        )

    tap_copies = [tap_copy(lax.rem(ring + step, rings), step) for step in range(1, rings)]
    for copy in tap_copies:
        copy.start()
    summed = [mine[b] for b in range(2)]
    for step, copy in enumerate(tap_copies):
        copy.wait_recv()
        summed = [summed[b] + others[step + 1, b] for b in range(2)]
    gate_taps[...] = summed[0][:taps] * norm_factor
    value_taps[...] = summed[1][:taps] * norm_factor

    for copy in tap_copies:
        copy.wait_send()
    send_all(lambda copy: copy.wait_send())
    for target in targets:
        for p in range(pieces):
            exchange(target, p, base_at).wait_send()


def quad_kernel(
    rings, taps, norm_factor,
    gate_in, value_in, filter_gate, filter_value, teacher_in,
    gate_out, value_out, gate_taps, value_taps,
    raw_g, raw_v, conv_g, conv_v, hid, nrm, teach, perm, keep,
    s1, r1, s2, r2, res, gbuf, hgrad, lane_sums, small, invc,
    sums, mine, others,
    in_sem, s1_send, s1_recv, s2_send, s2_recv, ag_send, ag_recv,
    small_send, small_recv, tap_send, tap_recv,
):
    groups = 4
    length, width = gate_in.shape[1:]
    stripe, full = length // groups, width * groups
    factor = 16.0 / math.sqrt(length)
    blocks = length // BLK
    half, quarter, eighth = BLK // 2, BLK // 4, BLK // 8
    lanes = [slice(k, k + 128) for k in range(0, width, 128)]
    f32, bf16 = jnp.float32, jnp.bfloat16
    me, ring = lax.axis_index("chan"), lax.axis_index("seq")
    x, y = lax.rem(me, 2), me // 2
    across, along, diagonal = me + 1 - 2 * x, lax.rem(me + 2, 4), 3 - me
    offset = [BLK * (l * (l + 1) // 2) for l in range(blocks)]

    def rows(start, size, unit=None):
        return pl.ds(pl.multiple_of(start, unit or size), size)

    def push(src, dst, send, recv, to):
        return pltpu.make_async_remote_copy(
            src_ref=src, dst_ref=dst, send_sem=send, recv_sem=recv,
            device_id=(ring, to), device_id_type=MESH,
        )

    in_copies = []
    for l in range(blocks):
        for k, (src, dst) in enumerate(((gate_in, raw_g), (value_in, raw_v))):
            in_copies.append(pltpu.make_async_copy(
                src.at[0, pl.ds(l * BLK, BLK)], dst.at[pl.ds(PAD + l * BLK, BLK)], in_sem.at[k, l]
            ))
    for copy in in_copies:
        copy.start()
    teach_copy = pltpu.make_async_copy(teacher_in.at[0], teach, in_sem.at[2, 0])
    teach_copy.start()

    barrier = pltpu.get_barrier_semaphore()
    for to in (across, along, diagonal):
        pl.semaphore_signal(barrier, inc=1, device_id=(ring, to), device_id_type=MESH)
    for step in range(1, rings):
        pl.semaphore_signal(barrier, inc=1, device_id=(lax.rem(ring + step, rings), me), device_id_type=MESH)

    raw_g[0:PAD] = jnp.zeros((PAD, width), bf16)
    raw_v[0:PAD] = jnp.zeros((PAD, width), bf16)
    conv_g[length:] = jnp.zeros((PAD, width), f32)
    conv_v[length:] = jnp.zeros((PAD, width), f32)
    hgrad[length:] = jnp.zeros((PAD, width), f32)
    sums[...] = jnp.zeros(sums.shape, f32)

    def share(kind, l):
        small[kind, me, l] = jnp.broadcast_to(jnp.sum(lane_sums[...].T, axis=0, keepdims=True), (8, BLK))
        for k, to in enumerate((across, along, diagonal)):
            here = small.at[kind, me, l]
            push(here, here, small_send.at[kind, k, l], small_recv.at[kind, me, l], to).start()

    def total(kind, l):
        for o in (across, along, diagonal):
            there = small.at[kind, o, l]
            push(there, there, small_send.at[kind, 0, l], small_recv.at[kind, o, l], o).wait_recv()
        return small[kind, 0, l, 0:1] + small[kind, 1, l, 0:1] + small[kind, 2, l, 0:1] + small[kind, 3, l, 0:1]

    def column(row):
        return jnp.broadcast_to(row, (128, BLK)).T

    def conv(l):
        in_copies[2 * l].wait()
        in_copies[2 * l + 1].wait()

        def body(i, _):
            base = pl.multiple_of(l * BLK + i * TILE, TILE)
            squares = jnp.zeros((TILE, 128), f32)
            for lane in lanes:
                made = []
                for raw, weights, store in ((raw_g, filter_gate, conv_g), (raw_v, filter_value, conv_v)):
                    window = raw[pl.ds(base, TILE + PAD), lane].astype(f32)
                    out = weights[0:1, lane] * window[PAD:]
                    for j in range(1, taps):
                        out = out + weights[j : j + 1, lane] * pltpu.roll(window, j, 0)[PAD:]
                    store[pl.ds(base, TILE), lane] = out
                    made.append(out)
                hidden = (made[0] * made[1]).astype(bf16)
                hid[pl.ds(base, TILE), lane] = hidden
                hidden = hidden.astype(f32)
                squares = squares + hidden * hidden
            lane_sums[pl.ds(pl.multiple_of(i * TILE, TILE), TILE)] = squares
            return 0

        lax.fori_loop(0, BLK // TILE, body, 0)

    def normalize(l):
        invc[pl.ds(l * BLK, BLK)] = column(lax.rsqrt(total(0, l) / full + epsilon))

        def body(i, _):
            base = pl.multiple_of(l * BLK + i * TILE, TILE)
            inverse = invc[pl.ds(base, TILE)]
            for lane in lanes:
                nrm[pl.ds(base, TILE), lane] = (hid[pl.ds(base, TILE), lane].astype(f32) * inverse).astype(bf16)
            return 0

        lax.fori_loop(0, BLK // TILE, body, 0)

    pieces = (quarter * (1 - x), half + quarter * (1 - y), quarter * x, half + quarter * y)

    def reach(l, k):
        return l * BLK + (half if k == 0 else BLK)

    def stage_one(l):
        for k, to in enumerate((across, along)):
            span = pl.ds(offset[l], reach(l, k))
            yield push(s1.at[k, :, span], r1.at[k, :, span], s1_send.at[k, l], s1_recv.at[k, l], to)

    def stage_two(l):
        for k, to in enumerate((across, along)):
            span = pl.ds(offset[l], reach(l, 1 - k))
            yield push(s2.at[k, :, span], r2.at[k, :, span], s2_send.at[k, l], s2_recv.at[k, l], to)

    def gram(l):
        for k, piece in enumerate(pieces):
            perm[k * quarter : (k + 1) * quarter] = nrm[rows(l * BLK + piece, quarter)]
        top = (l * BLK) % stripe
        held = jnp.where(me == (l * BLK) // stripe, 1.0, 0.0)

        def body(j, _):
            part = lax.dot_general(
                perm[...], nrm[rows(j * BLK, BLK)], (((1,), (1,)), ((), ())), preferred_element_type=f32
            ) / full
            cols = rows(offset[l] + j * BLK, BLK)
            for k, piece in enumerate(pieces):
                target = teach[rows(top + piece, quarter), rows(j * BLK, BLK)]
                apart = part[k * quarter : (k + 1) * quarter] - held * target
                if k < 2:
                    s1[k, :, cols] = apart.astype(bf16)
                else:
                    keep[k - 2, :, cols] = apart
            return 0

        lax.fori_loop(0, l + 1, body, 0)
        for copy in stage_one(l):
            copy.start()

    turns = ((0, y), (1, x))

    def combine(l):
        for copy in stage_one(l):
            copy.wait_recv()

        def add(k, own, cols):
            away = rows(eighth * (1 - own), eighth)
            s2[1 - k, :, cols] = (keep[k, away, cols] + r1[k, away, cols].astype(f32)).astype(bf16)

        def body(j, _):
            for k, own in turns:
                add(k, own, rows(offset[l] + j * BLK, BLK))
            return 0

        lax.fori_loop(0, l, body, 0)
        for k, own in turns:
            add(k, own, pl.ds(offset[l] + l * BLK, half if k == 0 else BLK))
        for copy in stage_two(l):
            copy.start()

    def place(l, k, px, py):
        return l * BLK + (quarter * px + eighth * py if k == 0 else half + quarter * py + eighth * px)

    def residue(l):
        for copy in stage_two(l):
            copy.wait_recv()

        def add(k, own, cols, dest):
            here = rows(eighth * own, eighth)
            apart = keep[k, here, cols] + r1[k, here, cols].astype(f32) + r2[1 - k, :, cols].astype(f32)
            res[rows(place(l, k, x, y), eighth), dest] = (factor * apart).astype(bf16)

        def body(j, _):
            for k, own in turns:
                add(k, own, rows(offset[l] + j * BLK, BLK), rows(j * BLK, BLK))
            return 0

        lax.fori_loop(0, l, body, 0)
        for k, own in turns:
            size = half if k == 0 else BLK
            add(k, own, pl.ds(offset[l] + l * BLK, size), pl.ds(l * BLK, size))

    def gather(l, slot, k, px, py, to):
        area = res.at[rows(place(l, k, px, py), eighth), pl.ds(0, reach(l, k))]
        return push(area, area, ag_send.at[slot, l], ag_recv.at[slot, l], to)

    def own_rows(l):
        return (
            gather(l, 0, 0, x, y, across), gather(l, 3, 1, x, y, along),
            gather(l, 1, 1, x, y, across), gather(l, 2, 0, x, y, along),
        )

    def relays(l):
        return gather(l, 4, 0, 1 - x, y, along), gather(l, 5, 1, x, 1 - y, across)

    def relay(l):
        first, second = relays(l)
        gather(l, 0, 0, 1 - x, y, across).wait_recv()
        first.start()
        gather(l, 3, 1, x, 1 - y, along).wait_recv()
        second.start()

    def landed(l):
        gather(l, 1, 1, 1 - x, y, across).wait_recv()
        gather(l, 2, 0, x, 1 - y, along).wait_recv()
        gather(l, 4, 0, 1 - x, 1 - y, along).wait_recv()
        gather(l, 5, 1, 1 - x, 1 - y, across).wait_recv()

    def lower(l):
        start, stop, mid = l * BLK, (l + 1) * BLK, l * BLK + half
        res[start:mid, mid:stop] = res[mid:stop, start:mid].T
        return jnp.dot(res[start:stop, 0:stop], nrm[0:stop], preferred_element_type=f32)

    def upper(l, begin, end):
        if begin == end:
            return 0.0
        return lax.dot_general(
            res[begin * BLK : end * BLK, l * BLK : (l + 1) * BLK], nrm[begin * BLK : end * BLK],
            (((0,), (0,)), ((), ())), preferred_element_type=f32,
        )

    def multiply(l):
        gbuf[l] = lower(l) + upper(l, l + 1, blocks)
        project(l)

    def prepare(l, late):
        gbuf[l] = lower(l) + upper(l, l + 1, late) + upper(l, late + 1, blocks)

    def complete(l, late):
        gbuf[l] += upper(l, late, late + 1)
        project(l)

    def project(l):
        def body(i, _):
            local = rows(i * TILE, TILE)
            at = rows(l * BLK + i * TILE, TILE)
            inner = jnp.zeros((TILE, 128), f32)
            for lane in lanes:
                inner = inner + hid[at, lane].astype(f32) * invc[at] * gbuf[l, local, lane]
            lane_sums[local] = inner
            return 0

        lax.fori_loop(0, BLK // TILE, body, 0)
        share(1, l)

    def finish(l):
        lane_sums[...] = column(total(1, l) / full)

        def body(i, _):
            local = rows(i * TILE, TILE)
            at = rows(l * BLK + i * TILE, TILE)
            inverse, projection = invc[at], lane_sums[local]
            for lane in lanes:
                normed = hid[at, lane].astype(f32) * inverse
                hgrad[at, lane] = inverse * (gbuf[l, local, lane] - normed * projection)
            return 0

        lax.fori_loop(0, BLK // TILE, body, 0)

    def back(l, tapped=True, stored=True):
        def body(i, _):
            base = pl.multiple_of(l * BLK + i * TILE, TILE)
            for lane in lanes:
                up = hgrad[pl.ds(base, TILE + PAD), lane]
                for b, (conv_by, raw, weights, store) in enumerate(
                    ((conv_v, raw_g, filter_gate, gate_out), (conv_g, raw_v, filter_value, value_out))
                ):
                    window = up * conv_by[pl.ds(base, TILE + PAD), lane]
                    signal = raw[pl.ds(pl.multiple_of(base + PAD, PAD), TILE), lane].astype(f32)
                    out = None
                    for j in range(taps):
                        shifted = (window if j == 0 else pltpu.roll(window, TILE + PAD - j, 0))[:TILE]
                        if stored:
                            term = weights[j : j + 1, lane] * shifted
                            out = term if out is None else out + term
                        if tapped:
                            product = shifted * signal
                            folded = product[0:8]
                            for r in range(8, TILE, 8):
                                folded = folded + product[r : r + 8]
                            sums[b, j, :, lane] += folded
                    if stored:
                        store[0, pl.ds(base, TILE), lane] = out.astype(bf16)
            return 0

        lax.fori_loop(0, BLK // TILE, body, 0)

    early = max(0, min(EARLY, blocks - 4))
    order = list(range(blocks - 1, early - 1, -1))
    order[:2] = order[1::-1]
    begin, hop = 2, 2
    for t in range(blocks + begin + 2 * hop):
        if t < blocks:
            conv(t)
            if t == 0:
                pl.semaphore_wait(barrier, groups + rings - 2)
            share(0, t)
        l = t - begin
        if l == 0:
            teach_copy.wait()
        if 0 <= l < blocks:
            normalize(l)
            gram(l)
        l = l - hop
        if 0 <= l < blocks:
            combine(l)
        l = l - hop
        if 0 <= l < blocks:
            residue(l)
            if l < early or l in order[:2]:
                for copy in own_rows(l):
                    copy.start()
        l = l - hop
        if 0 <= l < early:
            relay(l)

    def send_own(i):
        if i < len(order):
            for copy in own_rows(order[i]):
                copy.start()

    relay(order[0])
    send_own(2)
    ready = []
    for i, l in enumerate(order):
        final = i == len(order) - 1
        if final:
            for at in range(early):
                landed(at)
                prepare(at, l)
        if i:
            send_own(i + 2)
        if not final:
            relay(order[i + 1])
        landed(l)
        for at in [] if i == 0 and blocks > 1 else ([blocks - 1, blocks - 2] if i == 1 else [l]):
            multiply(at)
            ready.append(at)
            if len(ready) > LAG and not final:
                done = ready.pop(0)
                finish(done)
                back(done)
    for at in reversed(range(early)):
        complete(at, order[-1])
    while len(ready) > 1:
        done = ready.pop(0)
        finish(done)
        back(done)
    ready = ready + list(reversed(range(early)))
    for done in ready:
        finish(done)
    for done in ready:
        back(done, stored=not SPLIT)

    for b in range(2):
        for j in range(taps):
            mine[b, j : j + 1] = jnp.sum(sums[b, j], axis=0, keepdims=True)
        mine[b, taps:] = jnp.zeros((8 - taps, width), f32)

    tap_copies = [
        pltpu.make_async_remote_copy(
            src_ref=mine, dst_ref=others.at[step], send_sem=tap_send.at[step], recv_sem=tap_recv.at[step],
            device_id=(lax.rem(ring + step, rings), me), device_id_type=MESH,
        )
        for step in range(1, rings)
    ]
    for copy in tap_copies:
        copy.start()
    for done in ready if SPLIT else []:
        back(done, tapped=False)
    for l in range(blocks):
        for copy in (*stage_one(l), *stage_two(l), *own_rows(l), *relays(l)):
            copy.wait_send()
        for kind in range(2):
            for k, to in enumerate((across, along, diagonal)):
                here = small.at[kind, me, l]
                push(here, here, small_send.at[kind, k, l], small_recv.at[kind, me, l], to).wait_send()
    summed = [mine[b] for b in range(2)]
    for step, copy in enumerate(tap_copies):
        copy.wait_recv()
        summed = [summed[b] + others[step + 1, b] for b in range(2)]
    gate_taps[...] = summed[0][:taps] * norm_factor
    value_taps[...] = summed[1][:taps] * norm_factor
    for copy in tap_copies:
        copy.wait_send()


def quad_call(gate_raw, value_raw, filter_gate, filter_value, teacher):
    length, width = gate_raw.shape[1:]
    rings = lax.axis_size("seq")
    taps = filter_gate.shape[0]
    stripe, blocks = length // 4, length // BLK
    triangle = BLK * (blocks * (blocks + 1) // 2)
    norm_factor = 1.0 / math.sqrt(rings * length)
    f32, bf16 = jnp.float32, jnp.bfloat16
    any_space = pl.BlockSpec(memory_space=pl.ANY)
    vmem = pl.BlockSpec(memory_space=pltpu.VMEM)
    dma = pltpu.SemaphoreType.DMA
    made = pl.pallas_call(
        functools.partial(quad_kernel, rings, taps, norm_factor),
        out_shape=(
            pltpu.VMEM(gate_raw.shape, bf16),
            pltpu.VMEM(gate_raw.shape, bf16),
            pltpu.VMEM((taps, width), f32),
            pltpu.VMEM((taps, width), f32),
        ),
        in_specs=[any_space, any_space, vmem, vmem, any_space],
        out_specs=(vmem, vmem, vmem, vmem),
        scratch_shapes=[
            pltpu.VMEM((length + PAD, width), bf16),
            pltpu.VMEM((length + PAD, width), bf16),
            pltpu.VMEM((length + PAD, width), f32),
            pltpu.VMEM((length + PAD, width), f32),
            pltpu.VMEM((length, width), bf16),
            pltpu.VMEM((length, width), bf16),
            pltpu.VMEM((stripe, length), f32),
            pltpu.VMEM((BLK, width), bf16),
            pltpu.VMEM((2, BLK // 4, triangle), f32),
            pltpu.VMEM((2, BLK // 4, triangle), bf16),
            pltpu.VMEM((2, BLK // 4, triangle), bf16),
            pltpu.VMEM((2, BLK // 8, triangle), bf16),
            pltpu.VMEM((2, BLK // 8, triangle), bf16),
            pltpu.VMEM((length, length), bf16),
            pltpu.VMEM((blocks, BLK, width), f32),
            pltpu.VMEM((length + PAD, width), f32),
            pltpu.VMEM((BLK, 128), f32),
            pltpu.VMEM((2, 4, blocks, 8, BLK), f32),
            pltpu.VMEM((length, 128), f32),
            pltpu.VMEM((2, taps, 8, width), f32),
            pltpu.VMEM((2, 8, width), f32),
            pltpu.VMEM((rings, 2, 8, width), f32),
            dma((3, blocks)),
            dma((2, blocks)),
            dma((2, blocks)),
            dma((2, blocks)),
            dma((2, blocks)),
            dma((6, blocks)),
            dma((6, blocks)),
            dma((2, 3, blocks)),
            dma((2, 4, blocks)),
            dma((rings,)),
            dma((rings,)),
        ],
        compiler_params=pltpu.CompilerParams(
            collective_id=0, has_side_effects=True, vmem_limit_bytes=58 * 1024 * 1024
        ),
    )(gate_raw, value_raw, filter_gate, filter_value, teacher)
    return pl.pallas_call(
        store_kernel,
        out_shape=tuple(jax.ShapeDtypeStruct(array.shape, array.dtype) for array in made),
        in_specs=[vmem] * 4,
        out_specs=(any_space,) * 4,
        scratch_shapes=[dma((4,))],
        compiler_params=pltpu.CompilerParams(vmem_limit_bytes=1024 * 1024),
    )(*made)


def store_kernel(*refs):
    sems = refs[8]
    copies = [pltpu.make_async_copy(refs[k], refs[4 + k], sems.at[k]) for k in range(4)]
    for copy in copies:
        copy.start()
    for copy in copies:
        copy.wait()


def stripe_call(gate_raw, value_raw, filter_gate, filter_value, teacher):
    seq_count, length, width = gate_raw.shape
    groups, rings = lax.axis_size("chan"), lax.axis_size("seq")
    taps = filter_gate.shape[0]
    stripe, full = length // groups, width * groups
    norm_factor = 1.0 / math.sqrt(rings * seq_count * length)
    f32, bf16 = jnp.float32, jnp.bfloat16
    any_space = pl.BlockSpec(memory_space=pl.ANY)
    vmem = pl.BlockSpec(memory_space=pltpu.VMEM)
    dma = pltpu.SemaphoreType.DMA
    return pl.pallas_call(
        functools.partial(stripe_kernel, groups, rings, taps, norm_factor),
        out_shape=(
            pltpu.VMEM(gate_raw.shape, bf16),
            pltpu.VMEM(gate_raw.shape, bf16),
            jax.ShapeDtypeStruct((taps, width), f32),
            jax.ShapeDtypeStruct((taps, width), f32),
        ),
        in_specs=[any_space, any_space, vmem, vmem, any_space],
        out_specs=(vmem, vmem, vmem, vmem),
        scratch_shapes=[
            pltpu.VMEM((length + PAD, width), bf16),
            pltpu.VMEM((length + PAD, width), bf16),
            pltpu.VMEM((length + PAD, width), f32),
            pltpu.VMEM((length + PAD, width), f32),
            pltpu.VMEM((groups + 1, length, width), bf16),
            pltpu.VMEM((stripe, length), f32),
            pltpu.VMEM((stripe, full), bf16),
            pltpu.VMEM((stripe, full), bf16),
            pltpu.VMEM((stripe, full), f32),
            pltpu.VMEM((groups, stripe, width), bf16),
            pltpu.VMEM((length + PAD, width), bf16),
            pltpu.VMEM((2, taps, 8, width), f32),
            pltpu.VMEM((2, 8, width), f32),
            pltpu.VMEM((rings, 2, 8, width), f32),
            dma((3, groups)),
            dma((groups, groups)),
            dma((groups, groups)),
            dma((groups, 4)),
            dma((groups, 4)),
            dma((rings,)),
            dma((rings,)),
        ],
        compiler_params=pltpu.CompilerParams(
            collective_id=0, has_side_effects=True, vmem_limit_bytes=52 * 1024 * 1024
        ),
    )(gate_raw, value_raw, filter_gate, filter_value, teacher)


def on_device(gate_raw, value_raw, filter_gate, filter_value, teacher):
    length, width = gate_raw.shape[1:]
    groups = lax.axis_size("chan")
    square = groups == 4 and gate_raw.shape[0] == 1 and (length // 4) % BLK == 0 and width % 128 == 0
    call = quad_call if square else stripe_call
    return call(gate_raw, value_raw, filter_gate, filter_value, teacher)


def solution(mesh):
    placed = (
        P("seq", None, "chan"),
        P("seq", None, "chan"),
        P(None, "chan"),
        P(None, "chan"),
        P("seq", "chan", None),
    )
    return jax.shard_map(
        on_device,
        mesh=mesh,
        in_specs=placed,
        out_specs=(
            P("seq", None, "chan"),
            P("seq", None, "chan"),
            P(None, "chan"),
            P(None, "chan"),
        ),
        check_vma=False,
    )
```

```python
import functools
import math

import jax
import jax.numpy as jnp
from jax import lax
from jax.experimental import pallas as pl
from jax.experimental.pallas import tpu as pltpu
from jax.sharding import PartitionSpec as P

epsilon = 1e-06
PAD = 16
TILE = 64
BLK = 256
EARLY = 0
LAG = 2
SPLIT = True
MESH = pl.DeviceIdType.MESH


def stripe_kernel(
    groups, rings, taps, norm_factor,
    gate_in, value_in, filter_gate, filter_value, teacher_in,
    gate_out, value_out, gate_taps, value_taps,
    raw_g, raw_v, conv_g, conv_v, held, teach, own_n, block_n, total, outgoing, hgrad,
    sums, mine, others,
    in_sem, send_sem, recv_sem, a2a_send, a2a_recv, tap_send, tap_recv,
):
    length, width = gate_in.shape[1:]
    stripe = length // groups
    full = width * groups
    factor = 16.0 / math.sqrt(length)
    tile = min(TILE, stripe)
    lanes = [slice(k, min(k + 128, width)) for k in range(0, width, 128)]
    f32, bf16 = jnp.float32, jnp.bfloat16
    me, ring = lax.axis_index("chan"), lax.axis_index("seq")
    base_at, slot, proc = me, me, ring

    def rows_of(chunk, size=stripe, start=0):
        return pl.ds(pl.multiple_of(chunk * stripe + start, math.gcd(stripe, start) if start else stripe), size)

    in_copies = []
    for c in range(groups):
        span = pl.ds(c * stripe, stripe)
        dest = pl.ds(PAD + c * stripe, stripe)
        for k, (src, dst) in enumerate(((gate_in, raw_g), (value_in, raw_v))):
            in_copies.append(pltpu.make_async_copy(src.at[0, span], dst.at[dest], in_sem.at[k, c]))
    for copy in in_copies:
        copy.start()
    teach_copy = pltpu.make_async_copy(teacher_in.at[0], teach, in_sem.at[2, 0])
    teach_copy.start()

    barrier = pltpu.get_barrier_semaphore()
    for step in range(1, groups):
        pl.semaphore_signal(barrier, inc=1, device_id=(ring, lax.rem(me + step, groups)), device_id_type=MESH)
    greeted = groups + rings - 2
    for step in range(1, rings):
        pl.semaphore_signal(barrier, inc=1, device_id=(lax.rem(ring + step, rings), me), device_id_type=MESH)

    raw_g[0:PAD] = jnp.zeros((PAD, width), bf16)
    raw_v[0:PAD] = jnp.zeros((PAD, width), bf16)
    conv_g[length:] = jnp.zeros((PAD, width), f32)
    conv_v[length:] = jnp.zeros((PAD, width), f32)
    hgrad[length:] = jnp.zeros((PAD, width), bf16)
    sums[...] = jnp.zeros(sums.shape, f32)
    total[...] = jnp.zeros(total.shape, f32)
    for copy in in_copies:
        copy.wait()

    def conv_chunk(chunk):
        def body(i, _):
            base = pl.multiple_of(chunk * stripe + i * tile, tile)
            for lane in lanes:
                made = []
                for raw, weights, store in ((raw_g, filter_gate, conv_g), (raw_v, filter_value, conv_v)):
                    window = raw[pl.ds(base, tile + PAD), lane].astype(f32)
                    out = weights[0:1, lane] * window[PAD:]
                    for j in range(1, taps):
                        out = out + weights[j : j + 1, lane] * pltpu.roll(window, j, 0)[PAD:]
                    store[pl.ds(base, tile), lane] = out
                    made.append(out)
                held[slot, pl.ds(base, tile), lane] = (made[0] * made[1]).astype(bf16)
            return 0

        lax.fori_loop(0, stripe // tile, body, 0)

    def gather_copy(source, target, chunk, to, send):
        rows = rows_of(chunk)
        return pltpu.make_async_remote_copy(
            src_ref=held.at[source, rows], dst_ref=held.at[target, rows],
            send_sem=send, recv_sem=recv_sem.at[target, chunk],
            device_id=to, device_id_type=MESH,
        )

    def arrived(source, chunk):
        gather_copy(source, source, chunk, (ring, me), send_sem.at[0, 0]).wait_recv()

    for c in range(groups):
        conv_chunk(c)
    pl.semaphore_wait(barrier, greeted)

    def send_all(copy_do):
        def body(i, _):
            chunk, step = i // (groups - 1), 1 + lax.rem(i, groups - 1)
            copy_do(gather_copy(me, me, chunk, (ring, lax.rem(me + step, groups)), send_sem.at[step, chunk]))
            return 0

        lax.fori_loop(0, groups * (groups - 1), body, 0)

    send_all(lambda copy: copy.start())

    def wait_chunk(chunk):
        def body(step, _):
            arrived(lax.rem(me + step, groups), chunk)
            return 0

        lax.fori_loop(1, groups, body, 0)

    norm_tile = min(32, stripe)

    def scale_of(base):
        squares = jnp.zeros((norm_tile, width), f32)
        for g in range(groups):
            block = held[g, pl.ds(base, norm_tile)].astype(f32)
            squares = squares + block * block
        return lax.rsqrt(jnp.sum(squares, axis=1, keepdims=True) / full + epsilon)

    def normalize(chunk, dest):
        def body(i, _):
            base = pl.multiple_of(chunk * stripe + i * norm_tile, norm_tile)
            inverse = scale_of(base)
            for g in range(groups):
                block = held[g, pl.ds(base, norm_tile)].astype(f32)
                dest[pl.ds(pl.multiple_of(i * norm_tile, norm_tile), norm_tile), g * width : (g + 1) * width] = (
                    block * inverse
                ).astype(bf16)
            return 0

        lax.fori_loop(0, stripe // norm_tile, body, 0)

    teach_copy.wait()
    mat = min(256, stripe)

    def gram_chunk(t, _):
        chunk = lax.rem(me + t, groups)
        wait_chunk(chunk)
        normalize(chunk, block_n)

        @pl.when(t == 0)
        def _():
            own_n[...] = block_n[...]

        def body(m, _):
            rows = pl.ds(pl.multiple_of(m * mat, mat), mat)
            similarity = lax.dot_general(
                own_n[rows], block_n[...], (((1,), (1,)), ((), ())), preferred_element_type=f32
            ) / full
            residue = (factor * (similarity - teach[rows, rows_of(chunk)])).astype(bf16)
            total[rows] += jnp.dot(residue, block_n[...], preferred_element_type=f32)
            return 0

        lax.fori_loop(0, stripe // mat, body, 0)
        return 0

    lax.fori_loop(0, groups, gram_chunk, 0)

    def finish(i, _):
        local = pl.multiple_of(i * norm_tile, norm_tile)
        base = pl.multiple_of(base_at * stripe + i * norm_tile, norm_tile)
        rows = pl.ds(local, norm_tile)
        inverse = scale_of(base)
        inner = jnp.zeros((norm_tile, width), f32)
        for g in range(groups):
            part = slice(g * width, (g + 1) * width)
            inner = inner + held[g, pl.ds(base, norm_tile)].astype(f32) * inverse * total[rows, part]
        projection = jnp.sum(inner, axis=1, keepdims=True) / full
        for g in range(groups):
            part = slice(g * width, (g + 1) * width)
            normed = held[g, pl.ds(base, norm_tile)].astype(f32) * inverse
            outgoing[g, rows] = (inverse * (total[rows, part] - normed * projection)).astype(bf16)
        return 0

    pieces = max(1, min(4, stripe // 128))
    piece = stripe // pieces
    steps = piece // norm_tile

    def exchange(target, p, source_row):
        return pltpu.make_async_remote_copy(
            src_ref=outgoing.at[target, pl.ds(p * piece, piece)],
            dst_ref=hgrad.at[rows_of(source_row, piece, p * piece)],
            send_sem=a2a_send.at[target, p], recv_sem=a2a_recv.at[source_row, p],
            device_id=(proc, target), device_id_type=MESH,
        )

    targets = tuple(lax.rem(me + groups - step, groups) for step in range(1, groups))

    def stay(p):
        hgrad[rows_of(base_at, piece, p * piece)] = outgoing[me, pl.ds(p * piece, piece)]

    for p in reversed(range(pieces)):
        lax.fori_loop(p * steps, (p + 1) * steps, finish, 0)
        for target in targets:
            exchange(target, p, base_at).start()
        stay(p)

    def back_tile(base):
        for k in range(0, width, 128):
            lane = slice(k, min(k + 128, width))
            up = hgrad[pl.ds(base, tile + PAD), lane].astype(f32)
            for b, (conv, raw, weights, store) in enumerate(
                ((conv_v, raw_g, filter_gate, gate_out), (conv_g, raw_v, filter_value, value_out))
            ):
                window = up * conv[pl.ds(base, tile + PAD), lane]
                signal = raw[pl.ds(pl.multiple_of(base + PAD, PAD), tile), lane].astype(f32)
                out = None
                for j in range(taps):
                    shifted = (window if j == 0 else pltpu.roll(window, tile + PAD - j, 0))[:tile]
                    term = weights[j : j + 1, lane] * shifted
                    out = term if out is None else out + term
                    product = shifted * signal
                    folded = product[0:8]
                    for r in range(8, tile, 8):
                        folded = folded + product[r : r + 8]
                    sums[b, j, :, lane] += folded
                store[0, pl.ds(base, tile), lane] = out.astype(bf16)

    tiles = stripe // tile
    per = tiles // pieces
    sources = tuple(lax.rem(me + step, groups) for step in range(groups))
    for p in reversed(range(pieces)):
        for step, source in enumerate(sources):
            def landed(p=p, source=source):
                exchange(source, p, source).wait_recv()

            if step:
                landed()

            def inner_tiles(i, _, source=source):
                back_tile(pl.multiple_of(source * stripe + i * tile, tile))
                return 0

            lax.fori_loop(p * per, (p + 1) * per - (1 if p == pieces - 1 else 0), inner_tiles, 0)

    def last_tiles(c, _):
        back_tile(pl.multiple_of(c * stripe + (tiles - 1) * tile, tile))
        return 0

    lax.fori_loop(0, groups, last_tiles, 0)
    for b in range(2):
        for j in range(taps):
            mine[b, j : j + 1] = jnp.sum(sums[b, j], axis=0, keepdims=True)
        mine[b, taps:] = jnp.zeros((8 - taps, width), f32)

    def tap_copy(to, slot):
        return pltpu.make_async_remote_copy(
            src_ref=mine, dst_ref=others.at[slot], send_sem=tap_send.at[slot], recv_sem=tap_recv.at[slot],
            device_id=(to, me), device_id_type=MESH,
        )

    tap_copies = [tap_copy(lax.rem(ring + step, rings), step) for step in range(1, rings)]
    for copy in tap_copies:
        copy.start()
    summed = [mine[b] for b in range(2)]
    for step, copy in enumerate(tap_copies):
        copy.wait_recv()
        summed = [summed[b] + others[step + 1, b] for b in range(2)]
    gate_taps[...] = summed[0][:taps] * norm_factor
    value_taps[...] = summed[1][:taps] * norm_factor

    for copy in tap_copies:
        copy.wait_send()
    send_all(lambda copy: copy.wait_send())
    for target in targets:
        for p in range(pieces):
            exchange(target, p, base_at).wait_send()


def quad_kernel(
    rings, taps, norm_factor,
    gate_in, value_in, filter_gate, filter_value, teacher_in,
    gate_out, value_out, gate_taps, value_taps,
    raw_g, raw_v, conv_g, conv_v, hid, nrm, teach, perm, keep,
    s1, r1, s2, r2, res, gbuf, hgrad, lane_sums, small, invc,
    sums, mine, others,
    in_sem, s1_send, s1_recv, s2_send, s2_recv, ag_send, ag_recv,
    small_send, small_recv, tap_send, tap_recv,
):
    groups = 4
    length, width = gate_in.shape[1:]
    stripe, full = length // groups, width * groups
    factor = 16.0 / math.sqrt(length)
    blocks = length // BLK
    half, quarter, eighth = BLK // 2, BLK // 4, BLK // 8
    lanes = [slice(k, k + 128) for k in range(0, width, 128)]
    f32, bf16 = jnp.float32, jnp.bfloat16
    me, ring = lax.axis_index("chan"), lax.axis_index("seq")
    x, y = lax.rem(me, 2), me // 2
    across, along, diagonal = me + 1 - 2 * x, lax.rem(me + 2, 4), 3 - me
    offset = [BLK * (l * (l + 1) // 2) for l in range(blocks)]

    def rows(start, size, unit=None):
        return pl.ds(pl.multiple_of(start, unit or size), size)

    def push(src, dst, send, recv, to):
        return pltpu.make_async_remote_copy(
            src_ref=src, dst_ref=dst, send_sem=send, recv_sem=recv,
            device_id=(ring, to), device_id_type=MESH,
        )

    in_copies = []
    for l in range(blocks):
        for k, (src, dst) in enumerate(((gate_in, raw_g), (value_in, raw_v))):
            in_copies.append(pltpu.make_async_copy(
                src.at[0, pl.ds(l * BLK, BLK)], dst.at[pl.ds(PAD + l * BLK, BLK)], in_sem.at[k, l]
            ))
    for copy in in_copies:
        copy.start()
    teach_copy = pltpu.make_async_copy(teacher_in.at[0], teach, in_sem.at[2, 0])
    teach_copy.start()

    barrier = pltpu.get_barrier_semaphore()
    for to in (across, along, diagonal):
        pl.semaphore_signal(barrier, inc=1, device_id=(ring, to), device_id_type=MESH)
    for step in range(1, rings):
        pl.semaphore_signal(barrier, inc=1, device_id=(lax.rem(ring + step, rings), me), device_id_type=MESH)

    raw_g[0:PAD] = jnp.zeros((PAD, width), bf16)
    raw_v[0:PAD] = jnp.zeros((PAD, width), bf16)
    conv_g[length:] = jnp.zeros((PAD, width), f32)
    conv_v[length:] = jnp.zeros((PAD, width), f32)
    hgrad[length:] = jnp.zeros((PAD, width), f32)
    sums[...] = jnp.zeros(sums.shape, f32)

    def share(kind, l):
        small[kind, me, l] = jnp.broadcast_to(jnp.sum(lane_sums[...].T, axis=0, keepdims=True), (8, BLK))
        for k, to in enumerate((across, along, diagonal)):
            here = small.at[kind, me, l]
            push(here, here, small_send.at[kind, k, l], small_recv.at[kind, me, l], to).start()

    def total(kind, l):
        for o in (across, along, diagonal):
            there = small.at[kind, o, l]
            push(there, there, small_send.at[kind, 0, l], small_recv.at[kind, o, l], o).wait_recv()
        return small[kind, 0, l, 0:1] + small[kind, 1, l, 0:1] + small[kind, 2, l, 0:1] + small[kind, 3, l, 0:1]

    def column(row):
        return jnp.broadcast_to(row, (128, BLK)).T

    def conv(l):
        in_copies[2 * l].wait()
        in_copies[2 * l + 1].wait()

        def body(i, _):
            base = pl.multiple_of(l * BLK + i * TILE, TILE)
            squares = jnp.zeros((TILE, 128), f32)
            for lane in lanes:
                made = []
                for raw, weights, store in ((raw_g, filter_gate, conv_g), (raw_v, filter_value, conv_v)):
                    window = raw[pl.ds(base, TILE + PAD), lane].astype(f32)
                    out = weights[0:1, lane] * window[PAD:]
                    for j in range(1, taps):
                        out = out + weights[j : j + 1, lane] * pltpu.roll(window, j, 0)[PAD:]
                    store[pl.ds(base, TILE), lane] = out
                    made.append(out)
                hidden = (made[0] * made[1]).astype(bf16)
                hid[pl.ds(base, TILE), lane] = hidden
                hidden = hidden.astype(f32)
                squares = squares + hidden * hidden
            lane_sums[pl.ds(pl.multiple_of(i * TILE, TILE), TILE)] = squares
            return 0

        lax.fori_loop(0, BLK // TILE, body, 0)

    def normalize(l):
        invc[pl.ds(l * BLK, BLK)] = column(lax.rsqrt(total(0, l) / full + epsilon))

        def body(i, _):
            base = pl.multiple_of(l * BLK + i * TILE, TILE)
            inverse = invc[pl.ds(base, TILE)]
            for lane in lanes:
                nrm[pl.ds(base, TILE), lane] = (hid[pl.ds(base, TILE), lane].astype(f32) * inverse).astype(bf16)
            return 0

        lax.fori_loop(0, BLK // TILE, body, 0)

    pieces = (quarter * (1 - x), half + quarter * (1 - y), quarter * x, half + quarter * y)

    def reach(l, k):
        return l * BLK + (half if k == 0 else BLK)

    def stage_one(l):
        for k, to in enumerate((across, along)):
            span = pl.ds(offset[l], reach(l, k))
            yield push(s1.at[k, :, span], r1.at[k, :, span], s1_send.at[k, l], s1_recv.at[k, l], to)

    def stage_two(l):
        for k, to in enumerate((across, along)):
            span = pl.ds(offset[l], reach(l, 1 - k))
            yield push(s2.at[k, :, span], r2.at[k, :, span], s2_send.at[k, l], s2_recv.at[k, l], to)

    def gram(l):
        for k, piece in enumerate(pieces):
            perm[k * quarter : (k + 1) * quarter] = nrm[rows(l * BLK + piece, quarter)]
        top = (l * BLK) % stripe
        held = jnp.where(me == (l * BLK) // stripe, 1.0, 0.0)

        def body(j, _):
            part = lax.dot_general(
                perm[...], nrm[rows(j * BLK, BLK)], (((1,), (1,)), ((), ())), preferred_element_type=f32
            ) / full
            cols = rows(offset[l] + j * BLK, BLK)
            for k, piece in enumerate(pieces):
                target = teach[rows(top + piece, quarter), rows(j * BLK, BLK)]
                apart = part[k * quarter : (k + 1) * quarter] - held * target
                if k < 2:
                    s1[k, :, cols] = apart.astype(bf16)
                else:
                    keep[k - 2, :, cols] = apart
            return 0

        lax.fori_loop(0, l + 1, body, 0)
        for copy in stage_one(l):
            copy.start()

    turns = ((0, y), (1, x))

    def combine(l):
        for copy in stage_one(l):
            copy.wait_recv()

        def add(k, own, cols):
            away = rows(eighth * (1 - own), eighth)
            s2[1 - k, :, cols] = (keep[k, away, cols] + r1[k, away, cols].astype(f32)).astype(bf16)

        def body(j, _):
            for k, own in turns:
                add(k, own, rows(offset[l] + j * BLK, BLK))
            return 0

        lax.fori_loop(0, l, body, 0)
        for k, own in turns:
            add(k, own, pl.ds(offset[l] + l * BLK, half if k == 0 else BLK))
        for copy in stage_two(l):
            copy.start()

    def place(l, k, px, py):
        return l * BLK + (quarter * px + eighth * py if k == 0 else half + quarter * py + eighth * px)

    def residue(l):
        for copy in stage_two(l):
            copy.wait_recv()

        def add(k, own, cols, dest):
            here = rows(eighth * own, eighth)
            apart = keep[k, here, cols] + r1[k, here, cols].astype(f32) + r2[1 - k, :, cols].astype(f32)
            res[rows(place(l, k, x, y), eighth), dest] = (factor * apart).astype(bf16)

        def body(j, _):
            for k, own in turns:
                add(k, own, rows(offset[l] + j * BLK, BLK), rows(j * BLK, BLK))
            return 0

        lax.fori_loop(0, l, body, 0)
        for k, own in turns:
            size = half if k == 0 else BLK
            add(k, own, pl.ds(offset[l] + l * BLK, size), pl.ds(l * BLK, size))

    def gather(l, slot, k, px, py, to):
        area = res.at[rows(place(l, k, px, py), eighth), pl.ds(0, reach(l, k))]
        return push(area, area, ag_send.at[slot, l], ag_recv.at[slot, l], to)

    def own_rows(l):
        return (
            gather(l, 0, 0, x, y, across), gather(l, 3, 1, x, y, along),
            gather(l, 1, 1, x, y, across), gather(l, 2, 0, x, y, along),
        )

    def relays(l):
        return gather(l, 4, 0, 1 - x, y, along), gather(l, 5, 1, x, 1 - y, across)

    def relay(l):
        first, second = relays(l)
        gather(l, 0, 0, 1 - x, y, across).wait_recv()
        first.start()
        gather(l, 3, 1, x, 1 - y, along).wait_recv()
        second.start()

    def landed(l):
        gather(l, 1, 1, 1 - x, y, across).wait_recv()
        gather(l, 2, 0, x, 1 - y, along).wait_recv()
        gather(l, 4, 0, 1 - x, 1 - y, along).wait_recv()
        gather(l, 5, 1, 1 - x, 1 - y, across).wait_recv()

    def lower(l):
        start, stop, mid = l * BLK, (l + 1) * BLK, l * BLK + half
        res[start:mid, mid:stop] = res[mid:stop, start:mid].T
        return jnp.dot(res[start:stop, 0:stop], nrm[0:stop], preferred_element_type=f32)

    def upper(l, begin, end):
        if begin == end:
            return 0.0
        return lax.dot_general(
            res[begin * BLK : end * BLK, l * BLK : (l + 1) * BLK], nrm[begin * BLK : end * BLK],
            (((0,), (0,)), ((), ())), preferred_element_type=f32,
        )

    def multiply(l):
        gbuf[l] = lower(l) + upper(l, l + 1, blocks)
        project(l)

    def prepare(l, late):
        gbuf[l] = lower(l) + upper(l, l + 1, late) + upper(l, late + 1, blocks)

    def complete(l, late):
        gbuf[l] += upper(l, late, late + 1)
        project(l)

    def project(l):
        def body(i, _):
            local = rows(i * TILE, TILE)
            at = rows(l * BLK + i * TILE, TILE)
            inner = jnp.zeros((TILE, 128), f32)
            for lane in lanes:
                inner = inner + hid[at, lane].astype(f32) * invc[at] * gbuf[l, local, lane]
            lane_sums[local] = inner
            return 0

        lax.fori_loop(0, BLK // TILE, body, 0)
        share(1, l)

    def finish(l):
        lane_sums[...] = column(total(1, l) / full)

        def body(i, _):
            local = rows(i * TILE, TILE)
            at = rows(l * BLK + i * TILE, TILE)
            inverse, projection = invc[at], lane_sums[local]
            for lane in lanes:
                normed = hid[at, lane].astype(f32) * inverse
                hgrad[at, lane] = inverse * (gbuf[l, local, lane] - normed * projection)
            return 0

        lax.fori_loop(0, BLK // TILE, body, 0)

    def back(l, tapped=True, stored=True):
        def body(i, _):
            base = pl.multiple_of(l * BLK + i * TILE, TILE)
            for lane in lanes:
                up = hgrad[pl.ds(base, TILE + PAD), lane]
                for b, (conv_by, raw, weights, store) in enumerate(
                    ((conv_v, raw_g, filter_gate, gate_out), (conv_g, raw_v, filter_value, value_out))
                ):
                    window = up * conv_by[pl.ds(base, TILE + PAD), lane]
                    signal = raw[pl.ds(pl.multiple_of(base + PAD, PAD), TILE), lane].astype(f32)
                    out = None
                    for j in range(taps):
                        shifted = (window if j == 0 else pltpu.roll(window, TILE + PAD - j, 0))[:TILE]
                        if stored:
                            term = weights[j : j + 1, lane] * shifted
                            out = term if out is None else out + term
                        if tapped:
                            product = shifted * signal
                            folded = product[0:8]
                            for r in range(8, TILE, 8):
                                folded = folded + product[r : r + 8]
                            sums[b, j, :, lane] += folded
                    if stored:
                        store[0, pl.ds(base, TILE), lane] = out.astype(bf16)
            return 0

        lax.fori_loop(0, BLK // TILE, body, 0)

    early = max(0, min(EARLY, blocks - 4))
    order = list(range(blocks - 1, early - 1, -1))
    order[:2] = order[1::-1]
    begin, hop = 3, 3
    for t in range(blocks + begin + 2 * hop):
        if t < blocks:
            conv(t)
            if t == 0:
                pl.semaphore_wait(barrier, groups + rings - 2)
            share(0, t)
        l = t - begin
        if l == 0:
            teach_copy.wait()
        if 0 <= l < blocks:
            normalize(l)
            gram(l)
        l = l - hop
        if 0 <= l < blocks:
            combine(l)
        l = l - hop
        if 0 <= l < blocks:
            residue(l)
            if l < early or l in order[:2]:
                for copy in own_rows(l):
                    copy.start()
        l = l - hop
        if 0 <= l < early:
            relay(l)

    def send_own(i):
        if i < len(order):
            for copy in own_rows(order[i]):
                copy.start()

    relay(order[0])
    send_own(2)
    ready = []
    for i, l in enumerate(order):
        final = i == len(order) - 1
        if final:
            for at in range(early):
                landed(at)
                prepare(at, l)
        if i:
            send_own(i + 2)
        if not final:
            relay(order[i + 1])
        landed(l)
        for at in [] if i == 0 and blocks > 1 else ([blocks - 1, blocks - 2] if i == 1 else [l]):
            multiply(at)
            ready.append(at)
            if len(ready) > LAG and not final:
                done = ready.pop(0)
                finish(done)
                back(done)
    for at in reversed(range(early)):
        complete(at, order[-1])
    while len(ready) > 1:
        done = ready.pop(0)
        finish(done)
        back(done)
    ready = ready + list(reversed(range(early)))
    for done in ready:
        finish(done)
    for done in ready:
        back(done, stored=not SPLIT)

    for b in range(2):
        for j in range(taps):
            mine[b, j : j + 1] = jnp.sum(sums[b, j], axis=0, keepdims=True)
        mine[b, taps:] = jnp.zeros((8 - taps, width), f32)

    tap_copies = [
        pltpu.make_async_remote_copy(
            src_ref=mine, dst_ref=others.at[step], send_sem=tap_send.at[step], recv_sem=tap_recv.at[step],
            device_id=(lax.rem(ring + step, rings), me), device_id_type=MESH,
        )
        for step in range(1, rings)
    ]
    for copy in tap_copies:
        copy.start()
    for done in ready if SPLIT else []:
        back(done, tapped=False)
    for l in range(blocks):
        for copy in (*stage_one(l), *stage_two(l), *own_rows(l), *relays(l)):
            copy.wait_send()
        for kind in range(2):
            for k, to in enumerate((across, along, diagonal)):
                here = small.at[kind, me, l]
                push(here, here, small_send.at[kind, k, l], small_recv.at[kind, me, l], to).wait_send()
    summed = [mine[b] for b in range(2)]
    for step, copy in enumerate(tap_copies):
        copy.wait_recv()
        summed = [summed[b] + others[step + 1, b] for b in range(2)]
    gate_taps[...] = summed[0][:taps] * norm_factor
    value_taps[...] = summed[1][:taps] * norm_factor
    for copy in tap_copies:
        copy.wait_send()


def quad_call(gate_raw, value_raw, filter_gate, filter_value, teacher):
    length, width = gate_raw.shape[1:]
    rings = lax.axis_size("seq")
    taps = filter_gate.shape[0]
    stripe, blocks = length // 4, length // BLK
    triangle = BLK * (blocks * (blocks + 1) // 2)
    norm_factor = 1.0 / math.sqrt(rings * length)
    f32, bf16 = jnp.float32, jnp.bfloat16
    any_space = pl.BlockSpec(memory_space=pl.ANY)
    vmem = pl.BlockSpec(memory_space=pltpu.VMEM)
    dma = pltpu.SemaphoreType.DMA
    made = pl.pallas_call(
        functools.partial(quad_kernel, rings, taps, norm_factor),
        out_shape=(
            pltpu.VMEM(gate_raw.shape, bf16),
            pltpu.VMEM(gate_raw.shape, bf16),
            pltpu.VMEM((taps, width), f32),
            pltpu.VMEM((taps, width), f32),
        ),
        in_specs=[any_space, any_space, vmem, vmem, any_space],
        out_specs=(vmem, vmem, vmem, vmem),
        scratch_shapes=[
            pltpu.VMEM((length + PAD, width), bf16),
            pltpu.VMEM((length + PAD, width), bf16),
            pltpu.VMEM((length + PAD, width), f32),
            pltpu.VMEM((length + PAD, width), f32),
            pltpu.VMEM((length, width), bf16),
            pltpu.VMEM((length, width), bf16),
            pltpu.VMEM((stripe, length), f32),
            pltpu.VMEM((BLK, width), bf16),
            pltpu.VMEM((2, BLK // 4, triangle), f32),
            pltpu.VMEM((2, BLK // 4, triangle), bf16),
            pltpu.VMEM((2, BLK // 4, triangle), bf16),
            pltpu.VMEM((2, BLK // 8, triangle), bf16),
            pltpu.VMEM((2, BLK // 8, triangle), bf16),
            pltpu.VMEM((length, length), bf16),
            pltpu.VMEM((blocks, BLK, width), f32),
            pltpu.VMEM((length + PAD, width), f32),
            pltpu.VMEM((BLK, 128), f32),
            pltpu.VMEM((2, 4, blocks, 8, BLK), f32),
            pltpu.VMEM((length, 128), f32),
            pltpu.VMEM((2, taps, 8, width), f32),
            pltpu.VMEM((2, 8, width), f32),
            pltpu.VMEM((rings, 2, 8, width), f32),
            dma((3, blocks)),
            dma((2, blocks)),
            dma((2, blocks)),
            dma((2, blocks)),
            dma((2, blocks)),
            dma((6, blocks)),
            dma((6, blocks)),
            dma((2, 3, blocks)),
            dma((2, 4, blocks)),
            dma((rings,)),
            dma((rings,)),
        ],
        compiler_params=pltpu.CompilerParams(
            collective_id=0, has_side_effects=True, vmem_limit_bytes=58 * 1024 * 1024
        ),
    )(gate_raw, value_raw, filter_gate, filter_value, teacher)
    return pl.pallas_call(
        store_kernel,
        out_shape=tuple(jax.ShapeDtypeStruct(array.shape, array.dtype) for array in made),
        in_specs=[vmem] * 4,
        out_specs=(any_space,) * 4,
        scratch_shapes=[dma((4,))],
        compiler_params=pltpu.CompilerParams(vmem_limit_bytes=1024 * 1024),
    )(*made)


def store_kernel(*refs):
    sems = refs[8]
    copies = [pltpu.make_async_copy(refs[k], refs[4 + k], sems.at[k]) for k in range(4)]
    for copy in copies:
        copy.start()
    for copy in copies:
        copy.wait()


def stripe_call(gate_raw, value_raw, filter_gate, filter_value, teacher):
    seq_count, length, width = gate_raw.shape
    groups, rings = lax.axis_size("chan"), lax.axis_size("seq")
    taps = filter_gate.shape[0]
    stripe, full = length // groups, width * groups
    norm_factor = 1.0 / math.sqrt(rings * seq_count * length)
    f32, bf16 = jnp.float32, jnp.bfloat16
    any_space = pl.BlockSpec(memory_space=pl.ANY)
    vmem = pl.BlockSpec(memory_space=pltpu.VMEM)
    dma = pltpu.SemaphoreType.DMA
    return pl.pallas_call(
        functools.partial(stripe_kernel, groups, rings, taps, norm_factor),
        out_shape=(
            pltpu.VMEM(gate_raw.shape, bf16),
            pltpu.VMEM(gate_raw.shape, bf16),
            jax.ShapeDtypeStruct((taps, width), f32),
            jax.ShapeDtypeStruct((taps, width), f32),
        ),
        in_specs=[any_space, any_space, vmem, vmem, any_space],
        out_specs=(vmem, vmem, vmem, vmem),
        scratch_shapes=[
            pltpu.VMEM((length + PAD, width), bf16),
            pltpu.VMEM((length + PAD, width), bf16),
            pltpu.VMEM((length + PAD, width), f32),
            pltpu.VMEM((length + PAD, width), f32),
            pltpu.VMEM((groups + 1, length, width), bf16),
            pltpu.VMEM((stripe, length), f32),
            pltpu.VMEM((stripe, full), bf16),
            pltpu.VMEM((stripe, full), bf16),
            pltpu.VMEM((stripe, full), f32),
            pltpu.VMEM((groups, stripe, width), bf16),
            pltpu.VMEM((length + PAD, width), bf16),
            pltpu.VMEM((2, taps, 8, width), f32),
            pltpu.VMEM((2, 8, width), f32),
            pltpu.VMEM((rings, 2, 8, width), f32),
            dma((3, groups)),
            dma((groups, groups)),
            dma((groups, groups)),
            dma((groups, 4)),
            dma((groups, 4)),
            dma((rings,)),
            dma((rings,)),
        ],
        compiler_params=pltpu.CompilerParams(
            collective_id=0, has_side_effects=True, vmem_limit_bytes=52 * 1024 * 1024
        ),
    )(gate_raw, value_raw, filter_gate, filter_value, teacher)


def on_device(gate_raw, value_raw, filter_gate, filter_value, teacher):
    length, width = gate_raw.shape[1:]
    groups = lax.axis_size("chan")
    square = groups == 4 and gate_raw.shape[0] == 1 and (length // 4) % BLK == 0 and width % 128 == 0
    call = quad_call if square else stripe_call
    return call(gate_raw, value_raw, filter_gate, filter_value, teacher)


def solution(mesh):
    placed = (
        P("seq", None, "chan"),
        P("seq", None, "chan"),
        P(None, "chan"),
        P(None, "chan"),
        P("seq", "chan", None),
    )
    return jax.shard_map(
        on_device,
        mesh=mesh,
        in_specs=placed,
        out_specs=(
            P("seq", None, "chan"),
            P("seq", None, "chan"),
            P(None, "chan"),
            P(None, "chan"),
        ),
        check_vma=False,
    )
```

```python
import functools
import math

import jax
import jax.numpy as jnp
from jax import lax
from jax.experimental import pallas as pl
from jax.experimental.pallas import tpu as pltpu
from jax.sharding import PartitionSpec as P

epsilon = 1e-06
PAD = 16
TILE = 64
BLK = 256
EARLY = 0
LAG = 2
SPLIT = True
MESH = pl.DeviceIdType.MESH


def stripe_kernel(
    groups, rings, taps, norm_factor,
    gate_in, value_in, filter_gate, filter_value, teacher_in,
    gate_out, value_out, gate_taps, value_taps,
    raw_g, raw_v, conv_g, conv_v, held, teach, own_n, block_n, total, outgoing, hgrad,
    sums, mine, others,
    in_sem, send_sem, recv_sem, a2a_send, a2a_recv, tap_send, tap_recv,
):
    length, width = gate_in.shape[1:]
    stripe = length // groups
    full = width * groups
    factor = 16.0 / math.sqrt(length)
    tile = min(TILE, stripe)
    lanes = [slice(k, min(k + 128, width)) for k in range(0, width, 128)]
    f32, bf16 = jnp.float32, jnp.bfloat16
    me, ring = lax.axis_index("chan"), lax.axis_index("seq")
    base_at, slot, proc = me, me, ring

    def rows_of(chunk, size=stripe, start=0):
        return pl.ds(pl.multiple_of(chunk * stripe + start, math.gcd(stripe, start) if start else stripe), size)

    in_copies = []
    for c in range(groups):
        span = pl.ds(c * stripe, stripe)
        dest = pl.ds(PAD + c * stripe, stripe)
        for k, (src, dst) in enumerate(((gate_in, raw_g), (value_in, raw_v))):
            in_copies.append(pltpu.make_async_copy(src.at[0, span], dst.at[dest], in_sem.at[k, c]))
    for copy in in_copies:
        copy.start()
    teach_copy = pltpu.make_async_copy(teacher_in.at[0], teach, in_sem.at[2, 0])
    teach_copy.start()

    barrier = pltpu.get_barrier_semaphore()
    for step in range(1, groups):
        pl.semaphore_signal(barrier, inc=1, device_id=(ring, lax.rem(me + step, groups)), device_id_type=MESH)
    greeted = groups + rings - 2
    for step in range(1, rings):
        pl.semaphore_signal(barrier, inc=1, device_id=(lax.rem(ring + step, rings), me), device_id_type=MESH)

    raw_g[0:PAD] = jnp.zeros((PAD, width), bf16)
    raw_v[0:PAD] = jnp.zeros((PAD, width), bf16)
    conv_g[length:] = jnp.zeros((PAD, width), f32)
    conv_v[length:] = jnp.zeros((PAD, width), f32)
    hgrad[length:] = jnp.zeros((PAD, width), bf16)
    sums[...] = jnp.zeros(sums.shape, f32)
    total[...] = jnp.zeros(total.shape, f32)
    for copy in in_copies:
        copy.wait()

    def conv_chunk(chunk):
        def body(i, _):
            base = pl.multiple_of(chunk * stripe + i * tile, tile)
            for lane in lanes:
                made = []
                for raw, weights, store in ((raw_g, filter_gate, conv_g), (raw_v, filter_value, conv_v)):
                    window = raw[pl.ds(base, tile + PAD), lane].astype(f32)
                    out = weights[0:1, lane] * window[PAD:]
                    for j in range(1, taps):
                        out = out + weights[j : j + 1, lane] * pltpu.roll(window, j, 0)[PAD:]
                    store[pl.ds(base, tile), lane] = out
                    made.append(out)
                held[slot, pl.ds(base, tile), lane] = (made[0] * made[1]).astype(bf16)
            return 0

        lax.fori_loop(0, stripe // tile, body, 0)

    def gather_copy(source, target, chunk, to, send):
        rows = rows_of(chunk)
        return pltpu.make_async_remote_copy(
            src_ref=held.at[source, rows], dst_ref=held.at[target, rows],
            send_sem=send, recv_sem=recv_sem.at[target, chunk],
            device_id=to, device_id_type=MESH,
        )

    def arrived(source, chunk):
        gather_copy(source, source, chunk, (ring, me), send_sem.at[0, 0]).wait_recv()

    for c in range(groups):
        conv_chunk(c)
    pl.semaphore_wait(barrier, greeted)

    def send_all(copy_do):
        def body(i, _):
            chunk, step = i // (groups - 1), 1 + lax.rem(i, groups - 1)
            copy_do(gather_copy(me, me, chunk, (ring, lax.rem(me + step, groups)), send_sem.at[step, chunk]))
            return 0

        lax.fori_loop(0, groups * (groups - 1), body, 0)

    send_all(lambda copy: copy.start())

    def wait_chunk(chunk):
        def body(step, _):
            arrived(lax.rem(me + step, groups), chunk)
            return 0

        lax.fori_loop(1, groups, body, 0)

    norm_tile = min(32, stripe)

    def scale_of(base):
        squares = jnp.zeros((norm_tile, width), f32)
        for g in range(groups):
            block = held[g, pl.ds(base, norm_tile)].astype(f32)
            squares = squares + block * block
        return lax.rsqrt(jnp.sum(squares, axis=1, keepdims=True) / full + epsilon)

    def normalize(chunk, dest):
        def body(i, _):
            base = pl.multiple_of(chunk * stripe + i * norm_tile, norm_tile)
            inverse = scale_of(base)
            for g in range(groups):
                block = held[g, pl.ds(base, norm_tile)].astype(f32)
                dest[pl.ds(pl.multiple_of(i * norm_tile, norm_tile), norm_tile), g * width : (g + 1) * width] = (
                    block * inverse
                ).astype(bf16)
            return 0

        lax.fori_loop(0, stripe // norm_tile, body, 0)

    teach_copy.wait()
    mat = min(256, stripe)

    def gram_chunk(t, _):
        chunk = lax.rem(me + t, groups)
        wait_chunk(chunk)
        normalize(chunk, block_n)

        @pl.when(t == 0)
        def _():
            own_n[...] = block_n[...]

        def body(m, _):
            rows = pl.ds(pl.multiple_of(m * mat, mat), mat)
            similarity = lax.dot_general(
                own_n[rows], block_n[...], (((1,), (1,)), ((), ())), preferred_element_type=f32
            ) / full
            residue = (factor * (similarity - teach[rows, rows_of(chunk)])).astype(bf16)
            total[rows] += jnp.dot(residue, block_n[...], preferred_element_type=f32)
            return 0

        lax.fori_loop(0, stripe // mat, body, 0)
        return 0

    lax.fori_loop(0, groups, gram_chunk, 0)

    def finish(i, _):
        local = pl.multiple_of(i * norm_tile, norm_tile)
        base = pl.multiple_of(base_at * stripe + i * norm_tile, norm_tile)
        rows = pl.ds(local, norm_tile)
        inverse = scale_of(base)
        inner = jnp.zeros((norm_tile, width), f32)
        for g in range(groups):
            part = slice(g * width, (g + 1) * width)
            inner = inner + held[g, pl.ds(base, norm_tile)].astype(f32) * inverse * total[rows, part]
        projection = jnp.sum(inner, axis=1, keepdims=True) / full
        for g in range(groups):
            part = slice(g * width, (g + 1) * width)
            normed = held[g, pl.ds(base, norm_tile)].astype(f32) * inverse
            outgoing[g, rows] = (inverse * (total[rows, part] - normed * projection)).astype(bf16)
        return 0

    pieces = max(1, min(4, stripe // 128))
    piece = stripe // pieces
    steps = piece // norm_tile

    def exchange(target, p, source_row):
        return pltpu.make_async_remote_copy(
            src_ref=outgoing.at[target, pl.ds(p * piece, piece)],
            dst_ref=hgrad.at[rows_of(source_row, piece, p * piece)],
            send_sem=a2a_send.at[target, p], recv_sem=a2a_recv.at[source_row, p],
            device_id=(proc, target), device_id_type=MESH,
        )

    targets = tuple(lax.rem(me + groups - step, groups) for step in range(1, groups))

    def stay(p):
        hgrad[rows_of(base_at, piece, p * piece)] = outgoing[me, pl.ds(p * piece, piece)]

    for p in reversed(range(pieces)):
        lax.fori_loop(p * steps, (p + 1) * steps, finish, 0)
        for target in targets:
            exchange(target, p, base_at).start()
        stay(p)

    def back_tile(base):
        for k in range(0, width, 128):
            lane = slice(k, min(k + 128, width))
            up = hgrad[pl.ds(base, tile + PAD), lane].astype(f32)
            for b, (conv, raw, weights, store) in enumerate(
                ((conv_v, raw_g, filter_gate, gate_out), (conv_g, raw_v, filter_value, value_out))
            ):
                window = up * conv[pl.ds(base, tile + PAD), lane]
                signal = raw[pl.ds(pl.multiple_of(base + PAD, PAD), tile), lane].astype(f32)
                out = None
                for j in range(taps):
                    shifted = (window if j == 0 else pltpu.roll(window, tile + PAD - j, 0))[:tile]
                    term = weights[j : j + 1, lane] * shifted
                    out = term if out is None else out + term
                    product = shifted * signal
                    folded = product[0:8]
                    for r in range(8, tile, 8):
                        folded = folded + product[r : r + 8]
                    sums[b, j, :, lane] += folded
                store[0, pl.ds(base, tile), lane] = out.astype(bf16)

    tiles = stripe // tile
    per = tiles // pieces
    sources = tuple(lax.rem(me + step, groups) for step in range(groups))
    for p in reversed(range(pieces)):
        for step, source in enumerate(sources):
            def landed(p=p, source=source):
                exchange(source, p, source).wait_recv()

            if step:
                landed()

            def inner_tiles(i, _, source=source):
                back_tile(pl.multiple_of(source * stripe + i * tile, tile))
                return 0

            lax.fori_loop(p * per, (p + 1) * per - (1 if p == pieces - 1 else 0), inner_tiles, 0)

    def last_tiles(c, _):
        back_tile(pl.multiple_of(c * stripe + (tiles - 1) * tile, tile))
        return 0

    lax.fori_loop(0, groups, last_tiles, 0)
    for b in range(2):
        for j in range(taps):
            mine[b, j : j + 1] = jnp.sum(sums[b, j], axis=0, keepdims=True)
        mine[b, taps:] = jnp.zeros((8 - taps, width), f32)

    def tap_copy(to, slot):
        return pltpu.make_async_remote_copy(
            src_ref=mine, dst_ref=others.at[slot], send_sem=tap_send.at[slot], recv_sem=tap_recv.at[slot],
            device_id=(to, me), device_id_type=MESH,
        )

    tap_copies = [tap_copy(lax.rem(ring + step, rings), step) for step in range(1, rings)]
    for copy in tap_copies:
        copy.start()
    summed = [mine[b] for b in range(2)]
    for step, copy in enumerate(tap_copies):
        copy.wait_recv()
        summed = [summed[b] + others[step + 1, b] for b in range(2)]
    gate_taps[...] = summed[0][:taps] * norm_factor
    value_taps[...] = summed[1][:taps] * norm_factor

    for copy in tap_copies:
        copy.wait_send()
    send_all(lambda copy: copy.wait_send())
    for target in targets:
        for p in range(pieces):
            exchange(target, p, base_at).wait_send()


def quad_kernel(
    rings, taps, norm_factor,
    gate_in, value_in, filter_gate, filter_value, teacher_in,
    gate_out, value_out, gate_taps, value_taps,
    raw_g, raw_v, conv_g, conv_v, hid, nrm, teach, perm, keep,
    s1, r1, s2, r2, res, gbuf, hgrad, lane_sums, small, invc,
    sums, mine, others,
    in_sem, s1_send, s1_recv, s2_send, s2_recv, ag_send, ag_recv,
    small_send, small_recv, tap_send, tap_recv,
):
    groups = 4
    length, width = gate_in.shape[1:]
    stripe, full = length // groups, width * groups
    factor = 16.0 / math.sqrt(length)
    blocks = length // BLK
    half, quarter, eighth = BLK // 2, BLK // 4, BLK // 8
    lanes = [slice(k, k + 128) for k in range(0, width, 128)]
    f32, bf16 = jnp.float32, jnp.bfloat16
    me, ring = lax.axis_index("chan"), lax.axis_index("seq")
    x, y = lax.rem(me, 2), me // 2
    across, along, diagonal = me + 1 - 2 * x, lax.rem(me + 2, 4), 3 - me
    offset = [BLK * (l * (l + 1) // 2) for l in range(blocks)]

    def rows(start, size, unit=None):
        return pl.ds(pl.multiple_of(start, unit or size), size)

    def push(src, dst, send, recv, to):
        return pltpu.make_async_remote_copy(
            src_ref=src, dst_ref=dst, send_sem=send, recv_sem=recv,
            device_id=(ring, to), device_id_type=MESH,
        )

    in_copies = []
    for l in range(blocks):
        for k, (src, dst) in enumerate(((gate_in, raw_g), (value_in, raw_v))):
            in_copies.append(pltpu.make_async_copy(
                src.at[0, pl.ds(l * BLK, BLK)], dst.at[pl.ds(PAD + l * BLK, BLK)], in_sem.at[k, l]
            ))
    for copy in in_copies:
        copy.start()
    teach_copy = pltpu.make_async_copy(teacher_in.at[0], teach, in_sem.at[2, 0])
    teach_copy.start()

    barrier = pltpu.get_barrier_semaphore()
    for to in (across, along, diagonal):
        pl.semaphore_signal(barrier, inc=1, device_id=(ring, to), device_id_type=MESH)
    for step in range(1, rings):
        pl.semaphore_signal(barrier, inc=1, device_id=(lax.rem(ring + step, rings), me), device_id_type=MESH)

    raw_g[0:PAD] = jnp.zeros((PAD, width), bf16)
    raw_v[0:PAD] = jnp.zeros((PAD, width), bf16)
    conv_g[length:] = jnp.zeros((PAD, width), f32)
    conv_v[length:] = jnp.zeros((PAD, width), f32)
    hgrad[length:] = jnp.zeros((PAD, width), f32)
    sums[...] = jnp.zeros(sums.shape, f32)

    def share(kind, l):
        small[kind, me, l] = jnp.broadcast_to(jnp.sum(lane_sums[...].T, axis=0, keepdims=True), (8, BLK))
        for k, to in enumerate((across, along, diagonal)):
            here = small.at[kind, me, l]
            push(here, here, small_send.at[kind, k, l], small_recv.at[kind, me, l], to).start()

    def total(kind, l):
        for o in (across, along, diagonal):
            there = small.at[kind, o, l]
            push(there, there, small_send.at[kind, 0, l], small_recv.at[kind, o, l], o).wait_recv()
        return small[kind, 0, l, 0:1] + small[kind, 1, l, 0:1] + small[kind, 2, l, 0:1] + small[kind, 3, l, 0:1]

    def column(row):
        return jnp.broadcast_to(row, (128, BLK)).T

    def conv(l):
        in_copies[2 * l].wait()
        in_copies[2 * l + 1].wait()

        def body(i, _):
            base = pl.multiple_of(l * BLK + i * TILE, TILE)
            squares = jnp.zeros((TILE, 128), f32)
            for lane in lanes:
                made = []
                for raw, weights, store in ((raw_g, filter_gate, conv_g), (raw_v, filter_value, conv_v)):
                    window = raw[pl.ds(base, TILE + PAD), lane].astype(f32)
                    out = weights[0:1, lane] * window[PAD:]
                    for j in range(1, taps):
                        out = out + weights[j : j + 1, lane] * pltpu.roll(window, j, 0)[PAD:]
                    store[pl.ds(base, TILE), lane] = out
                    made.append(out)
                hidden = (made[0] * made[1]).astype(bf16)
                hid[pl.ds(base, TILE), lane] = hidden
                hidden = hidden.astype(f32)
                squares = squares + hidden * hidden
            lane_sums[pl.ds(pl.multiple_of(i * TILE, TILE), TILE)] = squares
            return 0

        lax.fori_loop(0, BLK // TILE, body, 0)

    def normalize(l):
        invc[pl.ds(l * BLK, BLK)] = column(lax.rsqrt(total(0, l) / full + epsilon))

        def body(i, _):
            base = pl.multiple_of(l * BLK + i * TILE, TILE)
            inverse = invc[pl.ds(base, TILE)]
            for lane in lanes:
                nrm[pl.ds(base, TILE), lane] = (hid[pl.ds(base, TILE), lane].astype(f32) * inverse).astype(bf16)
            return 0

        lax.fori_loop(0, BLK // TILE, body, 0)

    pieces = (quarter * (1 - x), half + quarter * (1 - y), quarter * x, half + quarter * y)

    def reach(l, k):
        return l * BLK + (half if k == 0 else BLK)

    def stage_one(l):
        for k, to in enumerate((across, along)):
            span = pl.ds(offset[l], reach(l, k))
            yield push(s1.at[k, :, span], r1.at[k, :, span], s1_send.at[k, l], s1_recv.at[k, l], to)

    def stage_two(l):
        for k, to in enumerate((across, along)):
            span = pl.ds(offset[l], reach(l, 1 - k))
            yield push(s2.at[k, :, span], r2.at[k, :, span], s2_send.at[k, l], s2_recv.at[k, l], to)

    def gram(l):
        for k, piece in enumerate(pieces):
            perm[k * quarter : (k + 1) * quarter] = nrm[rows(l * BLK + piece, quarter)]
        top = (l * BLK) % stripe
        held = jnp.where(me == (l * BLK) // stripe, 1.0, 0.0)

        def body(j, _):
            part = lax.dot_general(
                perm[...], nrm[rows(j * BLK, BLK)], (((1,), (1,)), ((), ())), preferred_element_type=f32
            ) / full
            cols = rows(offset[l] + j * BLK, BLK)
            for k, piece in enumerate(pieces):
                target = teach[rows(top + piece, quarter), rows(j * BLK, BLK)]
                apart = part[k * quarter : (k + 1) * quarter] - held * target
                if k < 2:
                    s1[k, :, cols] = apart.astype(bf16)
                else:
                    keep[k - 2, :, cols] = apart
            return 0

        lax.fori_loop(0, l + 1, body, 0)
        for copy in stage_one(l):
            copy.start()

    turns = ((0, y), (1, x))

    def combine(l):
        for copy in stage_one(l):
            copy.wait_recv()

        def add(k, own, cols):
            away = rows(eighth * (1 - own), eighth)
            s2[1 - k, :, cols] = (keep[k, away, cols] + r1[k, away, cols].astype(f32)).astype(bf16)

        def body(j, _):
            for k, own in turns:
                add(k, own, rows(offset[l] + j * BLK, BLK))
            return 0

        lax.fori_loop(0, l, body, 0)
        for k, own in turns:
            add(k, own, pl.ds(offset[l] + l * BLK, half if k == 0 else BLK))
        for copy in stage_two(l):
            copy.start()

    def place(l, k, px, py):
        return l * BLK + (quarter * px + eighth * py if k == 0 else half + quarter * py + eighth * px)

    def residue(l):
        for copy in stage_two(l):
            copy.wait_recv()

        def add(k, own, cols, dest):
            here = rows(eighth * own, eighth)
            apart = keep[k, here, cols] + r1[k, here, cols].astype(f32) + r2[1 - k, :, cols].astype(f32)
            res[rows(place(l, k, x, y), eighth), dest] = (factor * apart).astype(bf16)

        def body(j, _):
            for k, own in turns:
                add(k, own, rows(offset[l] + j * BLK, BLK), rows(j * BLK, BLK))
            return 0

        lax.fori_loop(0, l, body, 0)
        for k, own in turns:
            size = half if k == 0 else BLK
            add(k, own, pl.ds(offset[l] + l * BLK, size), pl.ds(l * BLK, size))

    def gather(l, slot, k, px, py, to):
        area = res.at[rows(place(l, k, px, py), eighth), pl.ds(0, reach(l, k))]
        return push(area, area, ag_send.at[slot, l], ag_recv.at[slot, l], to)

    def own_rows(l):
        return (
            gather(l, 0, 0, x, y, across), gather(l, 3, 1, x, y, along),
            gather(l, 1, 1, x, y, across), gather(l, 2, 0, x, y, along),
        )

    def relays(l):
        return gather(l, 4, 0, 1 - x, y, along), gather(l, 5, 1, x, 1 - y, across)

    def relay(l):
        first, second = relays(l)
        gather(l, 0, 0, 1 - x, y, across).wait_recv()
        first.start()
        gather(l, 3, 1, x, 1 - y, along).wait_recv()
        second.start()

    def landed(l):
        gather(l, 1, 1, 1 - x, y, across).wait_recv()
        gather(l, 2, 0, x, 1 - y, along).wait_recv()
        gather(l, 4, 0, 1 - x, 1 - y, along).wait_recv()
        gather(l, 5, 1, 1 - x, 1 - y, across).wait_recv()

    def lower(l):
        start, stop, mid = l * BLK, (l + 1) * BLK, l * BLK + half
        res[start:mid, mid:stop] = res[mid:stop, start:mid].T
        return jnp.dot(res[start:stop, 0:stop], nrm[0:stop], preferred_element_type=f32)

    def upper(l, begin, end):
        if begin == end:
            return 0.0
        return lax.dot_general(
            res[begin * BLK : end * BLK, l * BLK : (l + 1) * BLK], nrm[begin * BLK : end * BLK],
            (((0,), (0,)), ((), ())), preferred_element_type=f32,
        )

    def multiply(l):
        gbuf[l] = lower(l) + upper(l, l + 1, blocks)
        project(l)

    def prepare(l, late):
        gbuf[l] = lower(l) + upper(l, l + 1, late) + upper(l, late + 1, blocks)

    def complete(l, late):
        gbuf[l] += upper(l, late, late + 1)
        project(l)

    def project(l):
        def body(i, _):
            local = rows(i * TILE, TILE)
            at = rows(l * BLK + i * TILE, TILE)
            inner = jnp.zeros((TILE, 128), f32)
            for lane in lanes:
                inner = inner + hid[at, lane].astype(f32) * invc[at] * gbuf[l, local, lane]
            lane_sums[local] = inner
            return 0

        lax.fori_loop(0, BLK // TILE, body, 0)
        share(1, l)

    def finish(l):
        lane_sums[...] = column(total(1, l) / full)

        def body(i, _):
            local = rows(i * TILE, TILE)
            at = rows(l * BLK + i * TILE, TILE)
            inverse, projection = invc[at], lane_sums[local]
            for lane in lanes:
                normed = hid[at, lane].astype(f32) * inverse
                hgrad[at, lane] = inverse * (gbuf[l, local, lane] - normed * projection)
            return 0

        lax.fori_loop(0, BLK // TILE, body, 0)

    def back(l, tapped=True, stored=True):
        def body(i, _):
            base = pl.multiple_of(l * BLK + i * TILE, TILE)
            for lane in lanes:
                up = hgrad[pl.ds(base, TILE + PAD), lane]
                for b, (conv_by, raw, weights, store) in enumerate(
                    ((conv_v, raw_g, filter_gate, gate_out), (conv_g, raw_v, filter_value, value_out))
                ):
                    window = up * conv_by[pl.ds(base, TILE + PAD), lane]
                    signal = raw[pl.ds(pl.multiple_of(base + PAD, PAD), TILE), lane].astype(f32)
                    out = None
                    for j in range(taps):
                        shifted = (window if j == 0 else pltpu.roll(window, TILE + PAD - j, 0))[:TILE]
                        if stored:
                            term = weights[j : j + 1, lane] * shifted
                            out = term if out is None else out + term
                        if tapped:
                            product = shifted * signal
                            folded = product[0:8]
                            for r in range(8, TILE, 8):
                                folded = folded + product[r : r + 8]
                            sums[b, j, :, lane] += folded
                    if stored:
                        store[0, pl.ds(base, TILE), lane] = out.astype(bf16)
            return 0

        lax.fori_loop(0, BLK // TILE, body, 0)

    early = max(0, min(EARLY, blocks - 4))
    order = list(range(blocks - 1, early - 1, -1))
    order[:2] = order[1::-1]
    begin, hop = 3, 3
    for t in range(blocks + begin + 2 * hop):
        if t < blocks:
            conv(t)
            if t == 0:
                pl.semaphore_wait(barrier, groups + rings - 2)
            share(0, t)
        l = t - begin
        if l == 0:
            teach_copy.wait()
        if 0 <= l < blocks:
            normalize(l)
            gram(l)
        l = l - hop
        if 0 <= l < blocks:
            combine(l)
        l = l - hop
        if 0 <= l < blocks:
            residue(l)
            if l < early or l in order[:2]:
                for copy in own_rows(l):
                    copy.start()
        l = l - hop
        if 0 <= l < early:
            relay(l)

    def send_own(i):
        if i < len(order):
            for copy in own_rows(order[i]):
                copy.start()

    relay(order[0])
    send_own(2)
    ready = []
    for i, l in enumerate(order):
        final = i == len(order) - 1
        if final:
            for at in range(early):
                landed(at)
                prepare(at, l)
        if i:
            send_own(i + 2)
        if not final:
            relay(order[i + 1])
        landed(l)
        for at in [] if i == 0 and blocks > 1 else ([blocks - 1, blocks - 2] if i == 1 else [l]):
            multiply(at)
            ready.append(at)
            if len(ready) > LAG and not final:
                done = ready.pop(0)
                finish(done)
                back(done)
    for at in reversed(range(early)):
        complete(at, order[-1])
    while len(ready) > 2:
        done = ready.pop(0)
        finish(done)
        back(done)
    ready = ready + list(reversed(range(early)))
    for done in ready:
        finish(done)
        back(done, stored=not SPLIT)

    for b in range(2):
        for j in range(taps):
            mine[b, j : j + 1] = jnp.sum(sums[b, j], axis=0, keepdims=True)
        mine[b, taps:] = jnp.zeros((8 - taps, width), f32)

    tap_copies = [
        pltpu.make_async_remote_copy(
            src_ref=mine, dst_ref=others.at[step], send_sem=tap_send.at[step], recv_sem=tap_recv.at[step],
            device_id=(lax.rem(ring + step, rings), me), device_id_type=MESH,
        )
        for step in range(1, rings)
    ]
    for copy in tap_copies:
        copy.start()
    for done in ready if SPLIT else []:
        back(done, tapped=False)
    for l in range(blocks):
        for copy in (*stage_one(l), *stage_two(l), *own_rows(l), *relays(l)):
            copy.wait_send()
        for kind in range(2):
            for k, to in enumerate((across, along, diagonal)):
                here = small.at[kind, me, l]
                push(here, here, small_send.at[kind, k, l], small_recv.at[kind, me, l], to).wait_send()
    summed = [mine[b] for b in range(2)]
    for step, copy in enumerate(tap_copies):
        copy.wait_recv()
        summed = [summed[b] + others[step + 1, b] for b in range(2)]
    gate_taps[...] = summed[0][:taps] * norm_factor
    value_taps[...] = summed[1][:taps] * norm_factor
    for copy in tap_copies:
        copy.wait_send()


def quad_call(gate_raw, value_raw, filter_gate, filter_value, teacher):
    length, width = gate_raw.shape[1:]
    rings = lax.axis_size("seq")
    taps = filter_gate.shape[0]
    stripe, blocks = length // 4, length // BLK
    triangle = BLK * (blocks * (blocks + 1) // 2)
    norm_factor = 1.0 / math.sqrt(rings * length)
    f32, bf16 = jnp.float32, jnp.bfloat16
    any_space = pl.BlockSpec(memory_space=pl.ANY)
    vmem = pl.BlockSpec(memory_space=pltpu.VMEM)
    dma = pltpu.SemaphoreType.DMA
    made = pl.pallas_call(
        functools.partial(quad_kernel, rings, taps, norm_factor),
        out_shape=(
            pltpu.VMEM(gate_raw.shape, bf16),
            pltpu.VMEM(gate_raw.shape, bf16),
            pltpu.VMEM((taps, width), f32),
            pltpu.VMEM((taps, width), f32),
        ),
        in_specs=[any_space, any_space, vmem, vmem, any_space],
        out_specs=(vmem, vmem, vmem, vmem),
        scratch_shapes=[
            pltpu.VMEM((length + PAD, width), bf16),
            pltpu.VMEM((length + PAD, width), bf16),
            pltpu.VMEM((length + PAD, width), f32),
            pltpu.VMEM((length + PAD, width), f32),
            pltpu.VMEM((length, width), bf16),
            pltpu.VMEM((length, width), bf16),
            pltpu.VMEM((stripe, length), f32),
            pltpu.VMEM((BLK, width), bf16),
            pltpu.VMEM((2, BLK // 4, triangle), f32),
            pltpu.VMEM((2, BLK // 4, triangle), bf16),
            pltpu.VMEM((2, BLK // 4, triangle), bf16),
            pltpu.VMEM((2, BLK // 8, triangle), bf16),
            pltpu.VMEM((2, BLK // 8, triangle), bf16),
            pltpu.VMEM((length, length), bf16),
            pltpu.VMEM((blocks, BLK, width), f32),
            pltpu.VMEM((length + PAD, width), f32),
            pltpu.VMEM((BLK, 128), f32),
            pltpu.VMEM((2, 4, blocks, 8, BLK), f32),
            pltpu.VMEM((length, 128), f32),
            pltpu.VMEM((2, taps, 8, width), f32),
            pltpu.VMEM((2, 8, width), f32),
            pltpu.VMEM((rings, 2, 8, width), f32),
            dma((3, blocks)),
            dma((2, blocks)),
            dma((2, blocks)),
            dma((2, blocks)),
            dma((2, blocks)),
            dma((6, blocks)),
            dma((6, blocks)),
            dma((2, 3, blocks)),
            dma((2, 4, blocks)),
            dma((rings,)),
            dma((rings,)),
        ],
        compiler_params=pltpu.CompilerParams(
            collective_id=0, has_side_effects=True, vmem_limit_bytes=58 * 1024 * 1024
        ),
    )(gate_raw, value_raw, filter_gate, filter_value, teacher)
    return pl.pallas_call(
        store_kernel,
        out_shape=tuple(jax.ShapeDtypeStruct(array.shape, array.dtype) for array in made),
        in_specs=[vmem] * 4,
        out_specs=(any_space,) * 4,
        scratch_shapes=[dma((4,))],
        compiler_params=pltpu.CompilerParams(vmem_limit_bytes=1024 * 1024),
    )(*made)


def store_kernel(*refs):
    sems = refs[8]
    copies = [pltpu.make_async_copy(refs[k], refs[4 + k], sems.at[k]) for k in range(4)]
    for copy in copies:
        copy.start()
    for copy in copies:
        copy.wait()


def stripe_call(gate_raw, value_raw, filter_gate, filter_value, teacher):
    seq_count, length, width = gate_raw.shape
    groups, rings = lax.axis_size("chan"), lax.axis_size("seq")
    taps = filter_gate.shape[0]
    stripe, full = length // groups, width * groups
    norm_factor = 1.0 / math.sqrt(rings * seq_count * length)
    f32, bf16 = jnp.float32, jnp.bfloat16
    any_space = pl.BlockSpec(memory_space=pl.ANY)
    vmem = pl.BlockSpec(memory_space=pltpu.VMEM)
    dma = pltpu.SemaphoreType.DMA
    return pl.pallas_call(
        functools.partial(stripe_kernel, groups, rings, taps, norm_factor),
        out_shape=(
            pltpu.VMEM(gate_raw.shape, bf16),
            pltpu.VMEM(gate_raw.shape, bf16),
            jax.ShapeDtypeStruct((taps, width), f32),
            jax.ShapeDtypeStruct((taps, width), f32),
        ),
        in_specs=[any_space, any_space, vmem, vmem, any_space],
        out_specs=(vmem, vmem, vmem, vmem),
        scratch_shapes=[
            pltpu.VMEM((length + PAD, width), bf16),
            pltpu.VMEM((length + PAD, width), bf16),
            pltpu.VMEM((length + PAD, width), f32),
            pltpu.VMEM((length + PAD, width), f32),
            pltpu.VMEM((groups + 1, length, width), bf16),
            pltpu.VMEM((stripe, length), f32),
            pltpu.VMEM((stripe, full), bf16),
            pltpu.VMEM((stripe, full), bf16),
            pltpu.VMEM((stripe, full), f32),
            pltpu.VMEM((groups, stripe, width), bf16),
            pltpu.VMEM((length + PAD, width), bf16),
            pltpu.VMEM((2, taps, 8, width), f32),
            pltpu.VMEM((2, 8, width), f32),
            pltpu.VMEM((rings, 2, 8, width), f32),
            dma((3, groups)),
            dma((groups, groups)),
            dma((groups, groups)),
            dma((groups, 4)),
            dma((groups, 4)),
            dma((rings,)),
            dma((rings,)),
        ],
        compiler_params=pltpu.CompilerParams(
            collective_id=0, has_side_effects=True, vmem_limit_bytes=52 * 1024 * 1024
        ),
    )(gate_raw, value_raw, filter_gate, filter_value, teacher)


def on_device(gate_raw, value_raw, filter_gate, filter_value, teacher):
    length, width = gate_raw.shape[1:]
    groups = lax.axis_size("chan")
    square = groups == 4 and gate_raw.shape[0] == 1 and (length // 4) % BLK == 0 and width % 128 == 0
    call = quad_call if square else stripe_call
    return call(gate_raw, value_raw, filter_gate, filter_value, teacher)


def solution(mesh):
    placed = (
        P("seq", None, "chan"),
        P("seq", None, "chan"),
        P(None, "chan"),
        P(None, "chan"),
        P("seq", "chan", None),
    )
    return jax.shard_map(
        on_device,
        mesh=mesh,
        in_specs=placed,
        out_specs=(
            P("seq", None, "chan"),
            P("seq", None, "chan"),
            P(None, "chan"),
            P(None, "chan"),
        ),
        check_vma=False,
    )
```
